32 devices in a mesh: seq: 8 (over y, x, core), fsdp: 4 (over z).
Axes of the slice: x: 2, y: 2, z: 4, core: 2. Of those that a mesh axis runs over, the one named last changes fastest.
Arguments:
- hidden: bfloat16 [8192, 3584], P(('seq', 'fsdp')), may hold values from -6 to 6
- queries: bfloat16 [8192, 2048], P(('seq', 'fsdp')), may hold values from -360 to 360
- kv_weights: bfloat16 [2, 3584, 1024], P(None, 'fsdp'), may hold values from -0.09375 to 0.09375
- image_groups: int32 [8], P('seq'), may hold values 0 or 1
- doc_ids: int32 [8192], replicated, may hold values from 0 to 7, never falling along the last dimension, each value on 1 to 3072 neighbouring positions
Outputs:
- attended: bfloat16 [8192, 2048], P(('seq', 'fsdp'))
The draws below stay inside these ranges and needn't reach their ends.
Inputs may be any that keep to these rules, and one draw needn't show every extreme that they name: `image_groups`: 1 marks a group of image tokens. `doc_ids`: never falling along the tokens; every document has 1 to 3072 tokens and one has exactly that many.
All inputs are finite; a program needn't handle non-finite values.
Results may differ from the reference program's by a relative error of at most 0.0055.
The reference program's roundings to bfloat16 on the way (of `keys_values` and `weights`) count: a program that leaves them out, or rounds other values in their place, can miss the bound.
Values may be sent and summed in bfloat16 or wider, within the bound.
A program may use at most 128 MiB of HBM per device.

```python
import math
import jax
import jax.numpy as jnp
import numpy as np
from jax import lax

D = 3584
KVH = 4
HD = 128
QH = 16
ROWS = 256
SPAN = 3
TOKENS = 8192
DOCS = 8
N_SEQ = 8
N_FSDP = 4


def draw_queries(key, part):
    base = jnp.clip(jax.random.normal(key, (TOKENS, QH * HD), jnp.float32), -6.0, 6.0)
    return base.astype(jnp.bfloat16)


def set_ends(array, own_key, smallest, high):
    index_at = [jax.random.randint(jax.random.fold_in(own_key, axis), (), 0, length) for axis, length in enumerate(array.shape)]
    longest = array.shape.index(max(array.shape))
    neighbour = index_at[:longest] + [(index_at[longest] + 1) % array.shape[longest]] + index_at[longest + 1:]
    return array.at[tuple(index_at)].set(smallest).at[tuple(neighbour)].set(high)


def levels(key, extent, cuts, smallest, top_value):
    loudness, own = 1.0, jax.random.fold_in(key, 6)
    for axis_at, shards_of in cuts:
        heights = jnp.exp(jax.random.uniform(jax.random.fold_in(own, axis_at), (shards_of,), jnp.float32, smallest / len(cuts), top_value / len(cuts)))
        loudness = loudness * jnp.repeat(heights, extent[axis_at] // shards_of).reshape([-1 if axis == axis_at else 1 for axis in range(len(extent))])
    return loudness


def profile(count, total, most, slope):
    loads = [(1 << 20) // math.isqrt(rank ** slope) + 1 for rank in range(2, count + 1)]
    surplus, given = total - most - (count - 1), [1] * (count - 1)
    while surplus > 0:
        movable = [i for i in range(count - 1) if given[i] < most]
        pool, budget = sum([loads[i] for i in movable]), surplus
        for i in movable:
            more = min(most - given[i], max(1, budget * loads[i] // pool), surplus)
            given[i] = given[i] + more
            surplus = surplus - more
    return np.array([most] + given)


def uneven_parts(rng, number_of, total, bound, skew):
    if number_of == 2:
        one = jax.random.randint(rng, (), max(1, total - bound), min(bound, total - 1) + 1)
        return jnp.stack([one, total - one])
    tallies = jnp.asarray(profile(number_of, total, bound, skew), jnp.int32)
    couples = (number_of - 1) // 2
    donor, sink = tallies[1:1 + 2 * couples:2], tallies[2:2 + 2 * couples:2]
    margin = jnp.minimum(donor - 1, bound - sink)
    passed = jax.random.randint(jax.random.fold_in(rng, 1), (couples,), 0, 1 << 20) % (margin + 1)
    tallies = tallies.at[1:1 + 2 * couples:2].set(donor - passed).at[2:2 + 2 * couples:2].set(sink + passed)
    return tallies[jax.random.permutation(jax.random.fold_in(rng, 2), number_of)]


def centred(rng, extent, deviation, most, pieces=(), kind=jnp.bfloat16):
    drawn = deviation * jax.random.normal(rng, extent, jnp.float32)
    if pieces:
        drawn = drawn * levels(rng, extent, pieces, -0.22, 0.18)
    return jnp.clip(drawn, -most, most).astype(kind)


def setup_inputs(seed: int = 0) -> dict:
    keys = jax.random.split(jax.random.key(seed), 6)
    hidden = centred(keys[0], (TOKENS, D), 1.0, 6.0, ((0, 32),))
    queries = draw_queries(jax.random.fold_in(keys[5], 71), 0)
    kv_weights = centred(keys[2], (2, D, 2 * KVH * HD), D ** -0.5, 0.09375, ((1, 4),))
    image_groups = set_ends((jax.random.randint(keys[3], (N_SEQ,), 0, 3) < 1).astype(jnp.int32), jax.random.fold_in(keys[3], 1), 0, 1)
    doc_ids = jnp.searchsorted(jnp.cumsum(uneven_parts(keys[4], DOCS, TOKENS, SPAN * ROWS * N_FSDP, 2)), jnp.arange(TOKENS), side="right").astype(jnp.int32)
    return {"hidden": hidden, "queries": queries, "kv_weights": kv_weights, "image_groups": image_groups, "doc_ids": doc_ids}


def build_mask(query_pos, key_pos, doc_ids, is_image, own_start):
    key_doc = jnp.where(key_pos >= 0, doc_ids[jnp.maximum(key_pos, 0)], -1)
    query_doc = doc_ids[query_pos]
    same_doc = query_doc[:, None] == key_doc[None, :]
    earlier = key_pos[None, :] <= query_pos[:, None]
    own_image = jnp.logical_and(is_image, key_pos[None, :] >= own_start)
    return jnp.logical_and(same_doc, jnp.logical_or(earlier, own_image))

def attend(query_rows, keys_values, allowed):
    n_query = query_rows.shape[0]
    n_keys = keys_values.shape[0]
    per_group = QH // KVH
    score_scale = 1.0 / math.sqrt(HD)
    query_heads = query_rows.reshape(n_query, KVH, per_group, HD).transpose(1, 0, 2, 3)
    key_heads = keys_values[:, :KVH * HD].reshape(n_keys, KVH, HD).transpose(1, 0, 2)
    value_heads = keys_values[:, KVH * HD:].reshape(n_keys, KVH, HD).transpose(1, 0, 2)

    def one_head(operands):
        head_q, head_k, head_v = operands
        scores = jnp.einsum('rgd,kd->grk', head_q.astype(jnp.float32), head_k.astype(jnp.float32)) * score_scale
        scores = jnp.where(allowed[None], scores, -1e+30)
        highest = lax.optimization_barrier(jnp.max(scores, axis=-1, keepdims=True))
        weights = jnp.where(allowed[None], jnp.exp(scores - highest), 0.0)
        totals = lax.optimization_barrier(jnp.sum(weights, axis=-1))
        rounded = lax.optimization_barrier(weights.astype(jnp.bfloat16))
        summed = jnp.einsum('grk,kd->rgd', rounded.astype(jnp.float32), head_v.astype(jnp.float32))
        return (summed / jnp.transpose(totals)[:, :, None]).astype(jnp.bfloat16)
    mixed = lax.map(one_head, (query_heads, key_heads, value_heads))
    return mixed.transpose(1, 0, 2, 3).reshape(n_query, QH * HD)

def reference(hidden, queries, kv_weights, image_groups, doc_ids):
    block_len = TOKENS // N_SEQ
    kv_width = 2 * KVH * HD

    def project(group):
        block_hidden = lax.dynamic_slice_in_dim(hidden, group * block_len, block_len, 0)
        weight = lax.dynamic_index_in_dim(kv_weights, image_groups[group], 0, keepdims=False)
        return jnp.dot(block_hidden, weight, preferred_element_type=jnp.float32).astype(jnp.bfloat16)
    kv_blocks = lax.map(project, jnp.arange(N_SEQ, dtype=jnp.int32))
    padded = jnp.concatenate([jnp.zeros((SPAN, block_len, kv_width), kv_blocks.dtype), kv_blocks], 0)

    def one_block(group):
        query_rows = lax.dynamic_slice_in_dim(queries, group * block_len, block_len, 0)
        window = lax.dynamic_slice_in_dim(padded, group, SPAN + 1, 0).reshape((SPAN + 1) * block_len, kv_width)
        offsets = group - SPAN + jnp.arange(SPAN + 1, dtype=jnp.int32)
        key_pos = (offsets[:, None] * block_len + jnp.arange(block_len, dtype=jnp.int32)[None, :]).reshape(-1)
        query_pos = group * block_len + jnp.arange(block_len, dtype=jnp.int32)
        allowed = build_mask(query_pos, key_pos, doc_ids, image_groups[group] == 1, group * block_len)
        return attend(query_rows, window, allowed)
    attended = lax.map(one_block, jnp.arange(N_SEQ, dtype=jnp.int32))
    return attended.reshape(TOKENS, QH * HD)
```

```python
import functools
import math

import jax
import jax.numpy as jnp
from jax import lax
from jax.experimental import pallas as pl
from jax.experimental.pallas import tpu as pltpu
from jax.sharding import PartitionSpec as P

KVH = 4
HD = 128
QH = 16
SPAN = 3
NEG = -1e30
QUAD = KVH
PER = QH // KVH
WIDE = PER * HD
LINE = 128
MESH = pl.DeviceIdType.MESH


def flip(place, bits):
    out = place
    bit = 1
    while bit <= bits:
        if bits & bit:
            out = out + bit * (1 - 2 * (lax.div(place, bit) % 2))
        bit *= 2
    return out


def gather_kernel(
    seq, fsdp, parts, mod_ref, hidden_ref, w_ref, q_ref,
    kv_out, q_out, mod_out,
    hid, w, made, mods, q_own,
    local, hid_send, hid_recv, mod_send, mod_recv, q_send, q_recv,
    wz_send, wz_recv, wy_send, wy_recv, kz_send, kz_recv, ky_send, ky_recv, made_sem,
):
    s = lax.axis_index("seq")
    z = lax.axis_index("fsdp")
    h = s % QUAD
    side = lax.div(h, 2)
    carried = lax.div(s, QUAD) % 2
    base = s - h
    twin, across, diag, partner = flip(s, 1), flip(s, 2), flip(s, 3), flip(s, 4)
    ahead, behind = s + QUAD, s - QUAD
    has_ahead, has_behind = ahead < seq, behind >= 0
    step = hidden_ref.shape[0] // parts
    depth = w_ref.shape[1]
    lines = [(way, d) for d in range(1, fsdp) for way in (0, 1)]

    def exists(way, d):
        return z - d >= 0 if way == 0 else z + d <= fsdp - 1

    def source(way, d):
        return z - d if way == 0 else z + d

    def goes_on(way):
        return z + 1 <= fsdp - 1 if way == 0 else z >= 1

    def onward(way):
        return (s, z + 1) if way == 0 else (s, z - 1)

    def columns(head, half):
        return pl.ds(pl.multiple_of((half * KVH + head) * HD, HD), HD)

    def remote(src, dst, send, recv, device):
        return pltpu.make_async_remote_copy(
            src_ref=src, dst_ref=dst, send_sem=send, recv_sem=recv, device_id=device, device_id_type=MESH
        )

    keep = [pltpu.make_async_copy(hidden_ref, hid.at[h], local.at[0])]
    for m in range(2):
        for half in range(2):
            keep.append(
                pltpu.make_async_copy(
                    w_ref.at[m, :, columns(h, half)],
                    w.at[z, m, :, half * HD : (half + 1) * HD],
                    local.at[1 + 2 * m + half],
                )
            )
    q_in = pltpu.make_async_copy(q_ref.at[:, pl.ds(pl.multiple_of(h * WIDE, HD), WIDE)], q_own, local.at[5])
    q_keep = pltpu.make_async_copy(q_own, q_out.at[h], local.at[6])
    mod_in = pltpu.make_async_copy(mod_ref, mods.at[h], local.at[7])
    for copy in keep:
        copy.start()
    q_in.start()
    mod_in.start()

    barrier = pltpu.get_barrier_semaphore()
    near = [(twin, z), (across, z), (diag, z), (partner, z)]
    near += [((s + QUAD) % seq, z), ((s - QUAD + seq) % seq, z)]
    for device in near:
        pl.semaphore_signal(barrier, inc=1, device_id=device, device_id_type=MESH)
    for way in (0, 1):
        @pl.when(goes_on(way))
        def _(way=way):
            pl.semaphore_signal(barrier, inc=1, device_id=onward(way), device_id_type=MESH)
    both = (z >= 1).astype(jnp.int32) + (z <= fsdp - 2).astype(jnp.int32)
    pl.semaphore_wait(barrier, len(near) + both)

    def w_slot(zs, m, half):
        return w.at[zs, m, :, half * HD : (half + 1) * HD]

    def w_line(way, d, half):
        src = w_ref.at[carried, :, columns(h, half)] if d == 0 else w_slot(source(way, d), carried, half)
        zs = z if d == 0 else source(way, d)
        return remote(
            src, w_slot(zs, carried, half), wz_send.at[way, d, half], wz_recv.at[way, d + 1, half], onward(way)
        )

    def w_arrived(way, d, half):
        return remote(
            w_slot(source(way, d), carried, half), w_slot(source(way, d), carried, half),
            wz_send.at[way, d, half], wz_recv.at[way, d, half], (s, z),
        )

    def w_swap(way, d, half):
        slot = w_slot(source(way, d), carried, half)
        return remote(slot, slot, wy_send.at[way, d, half], wy_recv.at[way, d, half], (partner, z))

    def w_swapped(way, d, half):
        slot = w_slot(source(way, d), 1 - carried, half)
        return remote(slot, slot, wy_send.at[way, d, half], wy_recv.at[way, d, half], (partner, z))

    def rows(part):
        return slice(part * step, (part + 1) * step)

    def hid_to(which, device, part):
        return remote(
            hidden_ref.at[rows(part)], hid.at[h, rows(part)],
            hid_send.at[which, part], hid_recv.at[which, part], (device, z),
        )

    def hid_relay(part):
        slot = hid.at[across - base, rows(part)]
        return remote(slot, slot, hid_send.at[2, part], hid_recv.at[2, part], (twin, z))

    def hid_got(which, device, part):
        slot = hid.at[device - base, rows(part)]
        return remote(slot, slot, hid_send.at[which, part], hid_recv.at[which, part], (twin, z))

    mates = (twin, across, diag)

    def mod_to(i):
        return remote(mod_ref, mods.at[h], mod_send.at[i], mod_recv.at[i], (mates[i], z))

    def mod_got(i):
        slot = mods.at[mates[i] - base]
        return remote(slot, slot, mod_send.at[i], mod_recv.at[i], (mates[i], z))

    def q_to(i):
        head = mates[i] - base
        return remote(
            q_ref.at[:, pl.ds(pl.multiple_of(head * WIDE, HD), WIDE)], q_out.at[h],
            q_send.at[i], q_recv.at[i], (mates[i], z),
        )

    def q_got(i):
        slot = q_out.at[mates[i] - base]
        return remote(slot, slot, q_send.at[i], q_recv.at[i], (mates[i], z))

    def first_group(unit):
        return 2 * side if unit == 0 else 2 - 2 * side

    def kv_slot(unit, zs):
        return kv_out.at[:, pl.ds(SPAN + first_group(unit), 2), zs]

    def kv_line(unit, way, d):
        src = made.at[unit] if d == 0 else kv_slot(unit, source(way, d))
        zs = z if d == 0 else source(way, d)
        return remote(
            src, kv_slot(unit, zs), kz_send.at[unit, way, d], kz_recv.at[unit, way, d + 1], onward(way)
        )

    def kv_arrived(unit, way, d):
        slot = kv_slot(unit, source(way, d))
        return remote(slot, slot, kz_send.at[unit, way, d], kz_recv.at[unit, way, d], (s, z))

    def ahead_index(way, d):
        return 0 if d == 0 else 1 + 2 * (d - 1) + way

    def kv_ahead(unit, way, d, i):
        group = first_group(unit) + i
        zs = z if d == 0 else source(way, d)
        src = made.at[unit, :, pl.ds(i, 1)] if d == 0 else kv_out.at[:, pl.ds(SPAN + group, 1), zs]
        at = ahead_index(way, d)
        return remote(
            src, kv_out.at[:, pl.ds(group - 1, 1), zs],
            ky_send.at[unit, at, i], ky_recv.at[unit, at, i], (ahead, z),
        )

    def kv_behind(unit, way, d, i):
        group = first_group(unit) + i
        zs = z if d == 0 else source(way, d)
        slot = kv_out.at[:, pl.ds(group - 1, 1), zs]
        at = ahead_index(way, d)
        return remote(slot, slot, ky_send.at[unit, at, i], ky_recv.at[unit, at, i], (ahead, z))

    def kv_keep(unit):
        return pltpu.make_async_copy(made.at[unit], kv_slot(unit, z), made_sem.at[unit])

    def when(holds, act):
        @pl.when(holds)
        def _():
            act()

    for half in range(2):
        for way in (0, 1):
            when(goes_on(way), lambda: w_line(way, 0, half).start())
    for i in range(3):
        mod_to(i).start()
    for part in range(parts):
        hid_to(1, across, part).start()
    for part in range(parts):
        hid_to(0, twin, part).start()
    for i in (1, 2, 0):
        q_to(i).start()

    def pass_weights(way, d, half):
        def act():
            w_arrived(way, d, half).wait_recv()
            if d < fsdp - 1:
                when(goes_on(way), lambda: w_line(way, d, half).start())
            w_swap(way, d, half).start()

        when(exists(way, d), act)

    def pass_hidden(part):
        hid_got(1, across, part).wait_recv()
        hid_relay(part).start()

    def send_ahead(unit, way, d):
        for i in range(2):
            when(
                jnp.logical_and(has_ahead, first_group(unit) + i >= 1),
                lambda: kv_ahead(unit, way, d, i).start(),
            )

    def pass_kv(unit, way, d):
        def act():
            kv_arrived(unit, way, d).wait_recv()
            if d < fsdp - 1:
                when(goes_on(way), lambda: kv_line(unit, way, d).start())
            send_ahead(unit, way, d)

        when(exists(way, d), act)

    def project(unit):
        for i in range(2):
            group = first_group(unit) + i
            image = jnp.max(mods[group]) == 1
            total = None
            for zs in range(fsdp):
                weight = jnp.where(image, w[zs, 1], w[zs, 0])
                term = jnp.dot(
                    hid[group, :, zs * depth : (zs + 1) * depth], weight, preferred_element_type=jnp.float32
                )
                total = term if total is None else total + term
            rounded = total.astype(jnp.bfloat16)
            made[unit, 0, i] = rounded[:, :HD]
            made[unit, 1, i] = rounded[:, HD:]

    def send_made(unit):
        for way in (0, 1):
            when(goes_on(way), lambda: kv_line(unit, way, 0).start())
        send_ahead(unit, 0, 0)
        kv_keep(unit).start()

    done = 0
    for d in range(1, fsdp):
        for half in range(2):
            for way in (0, 1):
                pass_weights(way, d, half)
        if done < parts - 2:
            pass_hidden(done)
            done += 1
    for copy in keep:
        copy.wait()
    mod_in.wait()
    for i in range(3):
        mod_got(i).wait_recv()
    for part in range(parts):
        hid_got(0, twin, part).wait_recv()
    for way, d in lines:
        for half in range(2):
            when(exists(way, d), lambda: w_swapped(way, d, half).wait_recv())
    project(0)
    q_in.wait()
    q_keep.start()
    send_made(0)
    while done < parts:
        pass_hidden(done)
        done += 1
    for way in (0, 1):
        pass_kv(0, way, 1)
    for part in range(parts):
        hid_got(2, diag, part).wait_recv()
    project(1)
    for way in (0, 1):
        pass_kv(0, way, 2)
    send_made(1)
    for d in range(3, fsdp):
        for way in (0, 1):
            pass_kv(0, way, d)
    for d in range(1, fsdp):
        for way in (0, 1):
            pass_kv(1, way, d)
    mod_keep = pltpu.make_async_copy(mods, mod_out, local.at[8])
    mod_keep.start()
    for i in range(3):
        q_got(i).wait_recv()
    for unit in range(2):
        for way, d in [(0, 0)] + lines:
            for i in range(2):
                holds = jnp.logical_and(has_behind, first_group(unit) + i >= 1)
                if d:
                    holds = jnp.logical_and(holds, exists(way, d))
                when(holds, lambda: kv_behind(unit, way, d, i).wait_recv())

    mod_keep.wait()
    q_keep.wait()
    for unit in range(2):
        kv_keep(unit).wait()
    for half in range(2):
        for way in (0, 1):
            when(goes_on(way), lambda: w_line(way, 0, half).wait_send())
            for d in range(1, fsdp):
                def act(way=way, d=d, half=half):
                    if d < fsdp - 1:
                        when(goes_on(way), lambda: w_line(way, d, half).wait_send())
                    w_swap(way, d, half).wait_send()

                when(exists(way, d), act)
    for i in range(3):
        mod_to(i).wait_send()
        q_to(i).wait_send()
    for part in range(parts):
        hid_to(0, twin, part).wait_send()
        hid_to(1, across, part).wait_send()
        hid_relay(part).wait_send()

    def sent_ahead(unit, way, d):
        for i in range(2):
            when(
                jnp.logical_and(has_ahead, first_group(unit) + i >= 1),
                lambda: kv_ahead(unit, way, d, i).wait_send(),
            )

    for unit in range(2):
        for way in (0, 1):
            when(goes_on(way), lambda: kv_line(unit, way, 0).wait_send())
        sent_ahead(unit, 0, 0)
        for way, d in lines:
            def act(unit=unit, way=way, d=d):
                if d < fsdp - 1:
                    when(goes_on(way), lambda: kv_line(unit, way, d).wait_send())
                sent_ahead(unit, way, d)

            when(exists(way, d), act)


def gather(hidden, queries, kv_weights, image_groups):
    seq, fsdp = lax.axis_size("seq"), lax.axis_size("fsdp")
    rows, width = hidden.shape
    depth = kv_weights.shape[1]
    parts = 4
    marked = jnp.broadcast_to(image_groups[0], (8, LINE))
    anywhere = pl.BlockSpec(memory_space=pl.ANY)
    dma = pltpu.SemaphoreType.DMA
    bf16 = jnp.bfloat16
    return pl.pallas_call(
        functools.partial(gather_kernel, seq, fsdp, parts),
        in_specs=[anywhere] * 4,
        out_specs=[anywhere] * 3,
        out_shape=[
            jax.ShapeDtypeStruct((2, SPAN + QUAD, fsdp, rows, HD), bf16),
            jax.ShapeDtypeStruct((QUAD, rows, WIDE), bf16),
            jax.ShapeDtypeStruct((QUAD, 8, LINE), jnp.int32),
        ],
        scratch_shapes=[
            pltpu.VMEM((QUAD, rows, width), bf16),
            pltpu.VMEM((fsdp, 2, depth, 2 * HD), bf16),
            pltpu.VMEM((2, 2, 2, rows, HD), bf16),
            pltpu.VMEM((QUAD, 8, LINE), jnp.int32),
            pltpu.VMEM((rows, WIDE), bf16),
            dma((9,)),
            dma((3, parts)),
            dma((3, parts)),
            dma((3,)),
            dma((3,)),
            dma((3,)),
            dma((3,)),
            dma((2, fsdp, 2)),
            dma((2, fsdp + 1, 2)),
            dma((2, fsdp, 2)),
            dma((2, fsdp, 2)),
            dma((2, 2, fsdp)),
            dma((2, 2, fsdp + 1)),
            dma((2, 2 * fsdp, 2)),
            dma((2, 2 * fsdp, 2)),
            dma((2,)),
        ],
        compiler_params=pltpu.CompilerParams(
            collective_id=0, has_side_effects=True, vmem_limit_bytes=48 * 1024 * 1024
        ),
        name="gather",
    )(marked, hidden, kv_weights, queries)


def shifted(x, by, axis, fill):
    size = x.shape[axis]
    place = lax.broadcasted_iota(jnp.int32, x.shape, axis)
    moved = pltpu.roll(x, by % size, axis)
    inside = place >= by if by > 0 else place < size + by
    return jnp.where(inside, moved, fill)


def spread(x, pick, sign, fill):
    by = 1
    while by < x.shape[1]:
        x = pick(x, shifted(x, sign * by, 1, fill))
        by *= 2
    edge = x[:, -1:] if sign > 0 else x[:, :1]
    rows = shifted(jnp.broadcast_to(edge, x.shape), sign, 0, fill)
    by = 1
    while by < x.shape[0]:
        rows = pick(rows, shifted(rows, sign * by, 0, fill))
        by *= 2
    return pick(x, rows)


def bounds(docs):
    count = docs.shape[0] * docs.shape[1]
    place = (
        lax.broadcasted_iota(jnp.int32, docs.shape, 0) * docs.shape[1]
        + lax.broadcasted_iota(jnp.int32, docs.shape, 1)
    )
    lane = lax.broadcasted_iota(jnp.int32, docs.shape, 1)
    width = docs.shape[1]
    turned = pltpu.roll(docs, 1, 1)
    before = jnp.where(lane == 0, shifted(turned, 1, 0, -1), turned)
    turned = pltpu.roll(docs, width - 1, 1)
    after = jnp.where(lane == width - 1, shifted(turned, -1, 0, -1), turned)
    starts = jnp.where(docs != before, place, 0)
    ends = jnp.where(docs != after, place, count - 1)
    return spread(starts, jnp.maximum, 1, 0), spread(ends, jnp.minimum, -1, count - 1)


def attend_kernel(
    key_block, fsdp, docs_ref, mods_ref, q_ref, k_ref, v_ref, out_ref,
    starts, ends, lows, highs, qt, top, total, acc,
):
    rows = q_ref.shape[0]
    group = pl.program_id(0)
    block = rows * fsdp
    quad = lax.div(lax.axis_index("seq"), QUAD)

    @pl.when(group == 0)
    def _():
        starts[...], ends[...] = bounds(docs_ref[...])

    base = (quad * QUAD - SPAN) * block
    first_token = (quad * QUAD + group) * block
    first_query = first_token + lax.axis_index("fsdp") * rows
    image = mods_ref[:1, :] == 1
    for i in range(rows // LINE):
        line = lax.div(first_query, LINE) + i
        place = first_query + i * LINE + lax.broadcasted_iota(jnp.int32, (1, LINE), 1)
        last = jnp.minimum(ends[pl.ds(line, 1), :], first_token + block - 1)
        lows[:, i * LINE : (i + 1) * LINE] = starts[pl.ds(line, 1), :] - base
        highs[:, i * LINE : (i + 1) * LINE] = jnp.where(image, last, place) - base
    lo, hi = lows[...], highs[...]
    lo_min, lo_max, hi_min, hi_max = jnp.min(lo), jnp.max(lo), jnp.min(hi), jnp.max(hi)
    first = lax.div(lo_min, key_block)
    end = lax.div(hi_max, key_block) + 1
    full_first = jnp.minimum(lax.div(lo_max + key_block - 1, key_block), end)
    full_end = jnp.maximum(lax.div(hi_min + 1, key_block), full_first)

    lanes = [slice(g * rows, (g + 1) * rows) for g in range(PER)]
    factor = math.log2(math.e) / math.sqrt(HD)
    for g in range(PER):
        qt[:, g * rows : (g + 1) * rows] = q_ref[:, g * HD : (g + 1) * HD].T
    top[...] = jnp.full_like(top, NEG)
    total[...] = jnp.zeros_like(total)
    acc[...] = jnp.zeros_like(acc)

    def step(masked, b, _):
        at = pl.multiple_of(b * key_block, key_block)
        keys = k_ref[pl.ds(at, key_block), :]
        values = v_ref[pl.ds(at, key_block), :]
        if masked:
            place = at + lax.broadcasted_iota(jnp.int32, (key_block, rows), 0)
            allowed = jnp.logical_and(place >= lows[...], place <= highs[...])
        scores = [jnp.dot(keys, qt[:, at_g], preferred_element_type=jnp.float32) for at_g in lanes]
        if masked:
            scores = [jnp.where(allowed, score, NEG) for score in scores]
        before = [top[:, at_g] for at_g in lanes]
        peak = [
            jnp.maximum(old, jnp.max(score, axis=0, keepdims=True))
            for old, score in zip(before, scores)
        ]
        weights = [jnp.exp2((score - high) * factor) for score, high in zip(scores, peak)]
        shrink = [jnp.exp2((old - high) * factor) for old, high in zip(before, peak)]
        added = [jnp.sum(weight, axis=0, keepdims=True) for weight in weights]
        mixed = [
            lax.dot_general(
                values,
                weight.astype(jnp.bfloat16),
                (((0,), (0,)), ((), ())),
                preferred_element_type=jnp.float32,
            )
            for weight in weights
        ]
        for g, at_g in enumerate(lanes):
            top[:, at_g] = peak[g]
            total[:, at_g] = total[:, at_g] * shrink[g] + added[g]
            acc[:, at_g] = acc[:, at_g] * shrink[g] + mixed[g]
        return 0

    lax.fori_loop(first, full_first, functools.partial(step, True), 0)
    lax.fori_loop(full_first, full_end, functools.partial(step, False), 0)
    lax.fori_loop(full_end, end, functools.partial(step, True), 0)
    for g in range(PER):
        mixed = (acc[:, lanes[g]] / total[:, lanes[g]]).T
        out_ref[:, g * HD : (g + 1) * HD] = mixed.astype(out_ref.dtype)


def attend(kv, queries, mods, doc_ids):
    fsdp = lax.axis_size("fsdp")
    _, rows, wide = queries.shape
    n_keys = kv.shape[1] * kv.shape[2] * kv.shape[3]
    kv = kv.reshape(2, n_keys, HD)
    docs = doc_ids.reshape(-1, LINE)
    key_block = math.gcd(rows * fsdp, 512)
    whole = lambda j: (0, 0)
    return pl.pallas_call(
        functools.partial(attend_kernel, key_block, fsdp),
        grid=(QUAD,),
        in_specs=[
            pl.BlockSpec(docs.shape, whole),
            pl.BlockSpec((None, 8, LINE), lambda j: (j, 0, 0)),
            pl.BlockSpec((None, rows, wide), lambda j: (j, 0, 0)),
            pl.BlockSpec((None, n_keys, HD), lambda j: (0, 0, 0)),
            pl.BlockSpec((None, n_keys, HD), lambda j: (1, 0, 0)),
        ],
        out_specs=pl.BlockSpec((None, rows, wide), lambda j: (j, 0, 0)),
        out_shape=jax.ShapeDtypeStruct(queries.shape, queries.dtype),
        scratch_shapes=[
            pltpu.VMEM(docs.shape, jnp.int32),
            pltpu.VMEM(docs.shape, jnp.int32),
            pltpu.VMEM((1, rows), jnp.int32),
            pltpu.VMEM((1, rows), jnp.int32),
            pltpu.VMEM((HD, PER * rows), jnp.bfloat16),
            pltpu.VMEM((1, PER * rows), jnp.float32),
            pltpu.VMEM((1, PER * rows), jnp.float32),
            pltpu.VMEM((HD, PER * rows), jnp.float32),
        ],
        name="attend",
    )(docs, mods, queries, kv, kv)


def give_back_kernel(att_ref, out_ref, send, recv, local):
    s = lax.axis_index("seq")
    z = lax.axis_index("fsdp")
    h = s % QUAD
    base = s - h
    mates = (flip(s, 2), flip(s, 3), flip(s, 1))

    def at(head):
        return out_ref.at[:, pl.ds(pl.multiple_of(head * WIDE, HD), WIDE)]

    barrier = pltpu.get_barrier_semaphore()
    for mate in mates:
        pl.semaphore_signal(barrier, inc=1, device_id=(mate, z), device_id_type=MESH)
    keep = pltpu.make_async_copy(att_ref.at[h], at(h), local)
    keep.start()
    pl.semaphore_wait(barrier, len(mates))

    def give(i):
        return pltpu.make_async_remote_copy(
            src_ref=att_ref.at[mates[i] - base], dst_ref=at(h), send_sem=send.at[i], recv_sem=recv.at[i],
            device_id=(mates[i], z), device_id_type=MESH,
        )

    def got(i):
        slot = at(mates[i] - base)
        return pltpu.make_async_remote_copy(
            src_ref=slot, dst_ref=slot, send_sem=send.at[i], recv_sem=recv.at[i],
            device_id=(mates[i], z), device_id_type=MESH,
        )

    for i in range(3):
        give(i).start()
    for i in range(3):
        got(i).wait_recv()
    keep.wait()
    for i in range(3):
        give(i).wait_send()


def give_back(attended):
    _, rows, wide = attended.shape
    vmem = pl.BlockSpec(memory_space=pltpu.VMEM)
    return pl.pallas_call(
        give_back_kernel,
        in_specs=[vmem],
        out_specs=vmem,
        out_shape=jax.ShapeDtypeStruct((rows, QUAD * wide), attended.dtype),
        scratch_shapes=[
            pltpu.SemaphoreType.DMA((3,)),
            pltpu.SemaphoreType.DMA((3,)),
            pltpu.SemaphoreType.DMA,
        ],
        compiler_params=pltpu.CompilerParams(collective_id=1, has_side_effects=True),
        name="give_back",
    )(attended)


def local(hidden, queries, kv_weights, image_groups, doc_ids):
    kv, q, mods = gather(hidden, queries, kv_weights, image_groups)
    return give_back(attend(kv, q, mods, doc_ids))


def solution(mesh):
    in_specs = (
        P(("seq", "fsdp"), None),
        P(("seq", "fsdp"), None),
        P(None, "fsdp", None),
        P("seq"),
        P(),
    )
    out_specs = P(("seq", "fsdp"), None)
    return jax.shard_map(local, mesh=mesh, in_specs=in_specs, out_specs=out_specs, check_vma=False)
```

```python
import functools
import math

import jax
import jax.numpy as jnp
from jax import lax
from jax.experimental import pallas as pl
from jax.experimental.pallas import tpu as pltpu
from jax.sharding import PartitionSpec as P


KVH = 4
HD = 128
QH = 16
SPAN = 3
NEG = -1e30
QUAD = KVH
PER = QH // KVH
WIDE = PER * HD
LINE = 128
MESH = pl.DeviceIdType.MESH


def flip(place, bits):
    out = place
    bit = 1
    while bit <= bits:
        if bits & bit:
            out = out + bit * (1 - 2 * (lax.div(place, bit) % 2))
        bit *= 2
    return out


def gather_kernel(
    seq, fsdp, parts, mod_ref, docs_ref, hidden_ref, w_ref, q_ref,
    kv_out, q_out, limits,
    hid, w, made, mods, q_own, starts, ends,
    local, hid_send, hid_recv, mod_send, mod_recv, q_send, q_recv,
    wz_send, wz_recv, wy_send, wy_recv, kz_send, kz_recv, ky_send, ky_recv, made_sem,
):
    s = lax.axis_index("seq")
    z = lax.axis_index("fsdp")
    h = s % QUAD
    side = lax.div(h, 2)
    carried = lax.div(s, QUAD) % 2
    base = s - h
    twin, across, diag, partner = flip(s, 1), flip(s, 2), flip(s, 3), flip(s, 4)
    ahead, behind = s + QUAD, s - QUAD
    has_ahead, has_behind = ahead < seq, behind >= 0
    step = hidden_ref.shape[0] // parts
    depth = w_ref.shape[1]
    lines = [(way, d) for d in range(1, fsdp) for way in (0, 1)]

    def exists(way, d):
        return z - d >= 0 if way == 0 else z + d <= fsdp - 1

    def source(way, d):
        return z - d if way == 0 else z + d

    def goes_on(way):
        return z + 1 <= fsdp - 1 if way == 0 else z >= 1

    def onward(way):
        return (s, z + 1) if way == 0 else (s, z - 1)

    def columns(head, half):
        return pl.ds(pl.multiple_of((half * KVH + head) * HD, HD), HD)

    def remote(src, dst, send, recv, device):
        return pltpu.make_async_remote_copy(
            src_ref=src, dst_ref=dst, send_sem=send, recv_sem=recv, device_id=device, device_id_type=MESH
        )

    keep = [pltpu.make_async_copy(hidden_ref, hid.at[h], local.at[0])]
    for m in range(2):
        for half in range(2):
            keep.append(
                pltpu.make_async_copy(
                    w_ref.at[m, :, columns(h, half)],
                    w.at[z, m, :, half * HD : (half + 1) * HD],
                    local.at[1 + 2 * m + half],
                )
            )
    q_in = pltpu.make_async_copy(q_ref.at[:, pl.ds(pl.multiple_of(h * WIDE, HD), WIDE)], q_own, local.at[5])
    q_keep = pltpu.make_async_copy(q_own, q_out.at[0], local.at[6])
    mod_in = pltpu.make_async_copy(mod_ref, mods.at[h], local.at[7])
    for copy in keep:
        copy.start()
    q_in.start()
    mod_in.start()

    barrier = pltpu.get_barrier_semaphore()
    near = [(twin, z), (across, z), (diag, z), (partner, z)]
    near += [((s + QUAD) % seq, z), ((s - QUAD + seq) % seq, z)]
    for device in near:
        pl.semaphore_signal(barrier, inc=1, device_id=device, device_id_type=MESH)
    for way in (0, 1):
        @pl.when(goes_on(way))
        def _(way=way):
            pl.semaphore_signal(barrier, inc=1, device_id=onward(way), device_id_type=MESH)
    both = (z >= 1).astype(jnp.int32) + (z <= fsdp - 2).astype(jnp.int32)
    pl.semaphore_wait(barrier, len(near) + both)

    def w_slot(zs, m, half):
        return w.at[zs, m, :, half * HD : (half + 1) * HD]

    def w_line(way, d, half):
        src = w_ref.at[carried, :, columns(h, half)] if d == 0 else w_slot(source(way, d), carried, half)
        zs = z if d == 0 else source(way, d)
        return remote(
            src, w_slot(zs, carried, half), wz_send.at[way, d, half], wz_recv.at[way, d + 1, half], onward(way)
        )

    def w_arrived(way, d, half):
        return remote(
            w_slot(source(way, d), carried, half), w_slot(source(way, d), carried, half),
            wz_send.at[way, d, half], wz_recv.at[way, d, half], (s, z),
        )

    def w_swap(way, d, half):
        slot = w_slot(source(way, d), carried, half)
        return remote(slot, slot, wy_send.at[way, d, half], wy_recv.at[way, d, half], (partner, z))

    def w_swapped(way, d, half):
        slot = w_slot(source(way, d), 1 - carried, half)
        return remote(slot, slot, wy_send.at[way, d, half], wy_recv.at[way, d, half], (partner, z))

    def rows(part):
        return slice(part * step, (part + 1) * step)

    def hid_to(which, device, part):
        return remote(
            hidden_ref.at[rows(part)], hid.at[h, rows(part)],
            hid_send.at[which, part], hid_recv.at[which, part], (device, z),
        )

    def hid_relay(part):
        slot = hid.at[across - base, rows(part)]
        return remote(slot, slot, hid_send.at[2, part], hid_recv.at[2, part], (twin, z))

    def hid_got(which, device, part):
        slot = hid.at[device - base, rows(part)]
        return remote(slot, slot, hid_send.at[which, part], hid_recv.at[which, part], (twin, z))

    mates = (twin, across, diag)

    def mod_to(i):
        return remote(mod_ref, mods.at[h], mod_send.at[i], mod_recv.at[i], (mates[i], z))

    def mod_got(i):
        slot = mods.at[mates[i] - base]
        return remote(slot, slot, mod_send.at[i], mod_recv.at[i], (mates[i], z))

    def q_to(i):
        head = mates[i] - base
        return remote(
            q_ref.at[:, pl.ds(pl.multiple_of(head * WIDE, HD), WIDE)], q_out.at[1 + i],
            q_send.at[i], q_recv.at[i], (mates[i], z),
        )

    def q_got(i):
        slot = q_out.at[1 + i]
        return remote(slot, slot, q_send.at[i], q_recv.at[i], (mates[i], z))

    def first_group(unit):
        return 2 * side if unit == 0 else 2 - 2 * side

    def kv_slot(unit, zs):
        return kv_out.at[:, pl.ds(SPAN + first_group(unit), 2), zs]

    def kv_line(unit, way, d):
        src = made.at[unit] if d == 0 else kv_slot(unit, source(way, d))
        zs = z if d == 0 else source(way, d)
        return remote(
            src, kv_slot(unit, zs), kz_send.at[unit, way, d], kz_recv.at[unit, way, d + 1], onward(way)
        )

    def kv_arrived(unit, way, d):
        slot = kv_slot(unit, source(way, d))
        return remote(slot, slot, kz_send.at[unit, way, d], kz_recv.at[unit, way, d], (s, z))

    def ahead_index(way, d):
        return 0 if d == 0 else 1 + 2 * (d - 1) + way

    def kv_ahead(unit, way, d, i):
        group = first_group(unit) + i
        zs = z if d == 0 else source(way, d)
        src = made.at[unit, :, pl.ds(i, 1)] if d == 0 else kv_out.at[:, pl.ds(SPAN + group, 1), zs]
        at = ahead_index(way, d)
        return remote(
            src, kv_out.at[:, pl.ds(group - 1, 1), zs],
            ky_send.at[unit, at, i], ky_recv.at[unit, at, i], (ahead, z),
        )

    def kv_behind(unit, way, d, i):
        group = first_group(unit) + i
        zs = z if d == 0 else source(way, d)
        slot = kv_out.at[:, pl.ds(group - 1, 1), zs]
        at = ahead_index(way, d)
        return remote(slot, slot, ky_send.at[unit, at, i], ky_recv.at[unit, at, i], (ahead, z))

    def kv_keep(unit):
        return pltpu.make_async_copy(made.at[unit], kv_slot(unit, z), made_sem.at[unit])

    def when(holds, act):
        @pl.when(holds)
        def _():
            act()

    for half in range(2):
        for way in (0, 1):
            when(goes_on(way), lambda: w_line(way, 0, half).start())
    for i in range(3):
        mod_to(i).start()
    for part in range(parts):
        hid_to(1, across, part).start()
    for part in range(parts):
        hid_to(0, twin, part).start()
    for i in (1, 2, 0):
        q_to(i).start()

    def pass_weights(way, d, half):
        def act():
            w_arrived(way, d, half).wait_recv()
            if d < fsdp - 1:
                when(goes_on(way), lambda: w_line(way, d, half).start())
            w_swap(way, d, half).start()

        when(exists(way, d), act)

    def pass_hidden(part):
        hid_got(1, across, part).wait_recv()
        hid_relay(part).start()

    def send_ahead(unit, way, d):
        for i in range(2):
            when(
                jnp.logical_and(has_ahead, first_group(unit) + i >= 1),
                lambda: kv_ahead(unit, way, d, i).start(),
            )

    def pass_kv(unit, way, d):
        def act():
            kv_arrived(unit, way, d).wait_recv()
            if d < fsdp - 1:
                when(goes_on(way), lambda: kv_line(unit, way, d).start())
            send_ahead(unit, way, d)

        when(exists(way, d), act)

    def project(unit):
        for i in range(2):
            group = first_group(unit) + i
            image = jnp.max(mods[group]) == 1
            total = None
            for zs in range(fsdp):
                weight = jnp.where(image, w[zs, 1], w[zs, 0])
                term = jnp.dot(
                    hid[group, :, zs * depth : (zs + 1) * depth], weight, preferred_element_type=jnp.float32
                )
                total = term if total is None else total + term
            rounded = total.astype(jnp.bfloat16)
            made[unit, 0, i] = rounded[:, :HD]
            made[unit, 1, i] = rounded[:, HD:]

    def send_made(unit):
        for way in (0, 1):
            when(goes_on(way), lambda: kv_line(unit, way, 0).start())
        send_ahead(unit, 0, 0)
        kv_keep(unit).start()

    starts[...], ends[...] = bounds(docs_ref[...])
    mod_in.wait()
    for i in range(3):
        mod_got(i).wait_recv()
    block = hidden_ref.shape[0] * fsdp
    origin = (base - SPAN) * block
    for slot in range(QUAD):
        group = flip(s, slot)
        image = mods[group - base, :1] == 1
        for i in range(hidden_ref.shape[0] // LINE):
            first = group * block + z * hidden_ref.shape[0] + i * LINE
            line = lax.div(first, LINE)
            at = slice(i * LINE, (i + 1) * LINE)
            place = first + lax.broadcasted_iota(jnp.int32, (1, LINE), 1)
            last = jnp.minimum(ends[pl.ds(line, 1), :], group * block + block - 1)
            limits[slot : slot + 1, at] = starts[pl.ds(line, 1), :] - origin
            limits[QUAD + slot : QUAD + slot + 1, at] = jnp.where(image, last, place) - origin

    done = 0
    for d in range(1, fsdp):
        for half in range(2):
            for way in (0, 1):
                pass_weights(way, d, half)
        if done < parts - 2:
            pass_hidden(done)
            done += 1
    for copy in keep:
        copy.wait()
    for part in range(parts):
        hid_got(0, twin, part).wait_recv()
    for way, d in lines:
        for half in range(2):
            when(exists(way, d), lambda: w_swapped(way, d, half).wait_recv())
    project(0)
    q_in.wait()
    q_keep.start()
    send_made(0)
    while done < parts:
        pass_hidden(done)
        done += 1
    for way in (0, 1):
        pass_kv(0, way, 1)
    for part in range(parts):
        hid_got(2, diag, part).wait_recv()
    project(1)
    for way in (0, 1):
        pass_kv(0, way, 2)
    send_made(1)
    for d in range(3, fsdp):
        for way in (0, 1):
            pass_kv(0, way, d)
    for d in range(1, fsdp):
        for way in (0, 1):
            pass_kv(1, way, d)
    for i in range(3):
        q_got(i).wait_recv()
    for unit in range(2):
        for way, d in [(0, 0)] + lines:
            for i in range(2):
                holds = jnp.logical_and(has_behind, first_group(unit) + i >= 1)
                if d:
                    holds = jnp.logical_and(holds, exists(way, d))
                when(holds, lambda: kv_behind(unit, way, d, i).wait_recv())

    q_keep.wait()
    for unit in range(2):
        kv_keep(unit).wait()
    for half in range(2):
        for way in (0, 1):
            when(goes_on(way), lambda: w_line(way, 0, half).wait_send())
            for d in range(1, fsdp):
                def act(way=way, d=d, half=half):
                    if d < fsdp - 1:
                        when(goes_on(way), lambda: w_line(way, d, half).wait_send())
                    w_swap(way, d, half).wait_send()

                when(exists(way, d), act)
    for i in range(3):
        mod_to(i).wait_send()
        q_to(i).wait_send()
    for part in range(parts):
        hid_to(0, twin, part).wait_send()
        hid_to(1, across, part).wait_send()
        hid_relay(part).wait_send()

    def sent_ahead(unit, way, d):
        for i in range(2):
            when(
                jnp.logical_and(has_ahead, first_group(unit) + i >= 1),
                lambda: kv_ahead(unit, way, d, i).wait_send(),
            )

    for unit in range(2):
        for way in (0, 1):
            when(goes_on(way), lambda: kv_line(unit, way, 0).wait_send())
        sent_ahead(unit, 0, 0)
        for way, d in lines:
            def act(unit=unit, way=way, d=d):
                if d < fsdp - 1:
                    when(goes_on(way), lambda: kv_line(unit, way, d).wait_send())
                sent_ahead(unit, way, d)

            when(exists(way, d), act)


def shifted(x, by, axis, fill):
    size = x.shape[axis]
    place = lax.broadcasted_iota(jnp.int32, x.shape, axis)
    moved = pltpu.roll(x, by % size, axis)
    inside = place >= by if by > 0 else place < size + by
    return jnp.where(inside, moved, fill)


def spread(x, pick, sign, fill):
    by = 1
    while by < x.shape[1]:
        x = pick(x, shifted(x, sign * by, 1, fill))
        by *= 2
    edge = x[:, -1:] if sign > 0 else x[:, :1]
    rows = shifted(jnp.broadcast_to(edge, x.shape), sign, 0, fill)
    by = 1
    while by < x.shape[0]:
        rows = pick(rows, shifted(rows, sign * by, 0, fill))
        by *= 2
    return pick(x, rows)


def bounds(docs):
    count = docs.shape[0] * docs.shape[1]
    place = (
        lax.broadcasted_iota(jnp.int32, docs.shape, 0) * docs.shape[1]
        + lax.broadcasted_iota(jnp.int32, docs.shape, 1)
    )
    lane = lax.broadcasted_iota(jnp.int32, docs.shape, 1)
    width = docs.shape[1]
    turned = pltpu.roll(docs, 1, 1)
    before = jnp.where(lane == 0, shifted(turned, 1, 0, -1), turned)
    turned = pltpu.roll(docs, width - 1, 1)
    after = jnp.where(lane == width - 1, shifted(turned, -1, 0, -1), turned)
    starts = jnp.where(docs != before, place, 0)
    ends = jnp.where(docs != after, place, count - 1)
    return spread(starts, jnp.maximum, 1, 0), spread(ends, jnp.minimum, -1, count - 1)


def gather(hidden, queries, kv_weights, image_groups, doc_ids):
    seq, fsdp = lax.axis_size("seq"), lax.axis_size("fsdp")
    rows, width = hidden.shape
    depth = kv_weights.shape[1]
    parts = 4
    marked = jnp.broadcast_to(image_groups[0], (8, LINE))
    docs = doc_ids.reshape(-1, LINE)
    anywhere = pl.BlockSpec(memory_space=pl.ANY)
    far = pl.BlockSpec(memory_space=pltpu.HBM)
    vmem = pl.BlockSpec(memory_space=pltpu.VMEM)
    dma = pltpu.SemaphoreType.DMA
    bf16 = jnp.bfloat16
    return pl.pallas_call(
        functools.partial(gather_kernel, seq, fsdp, parts),
        in_specs=[far, vmem, far, far, far],
        out_specs=[anywhere, anywhere, vmem],
        out_shape=[
            jax.ShapeDtypeStruct((2, SPAN + QUAD, fsdp, rows, HD), bf16),
            jax.ShapeDtypeStruct((QUAD, rows, WIDE), bf16),
            jax.ShapeDtypeStruct((2 * QUAD, rows), jnp.int32),
        ],
        scratch_shapes=[
            pltpu.VMEM((QUAD, rows, width), bf16),
            pltpu.VMEM((fsdp, 2, depth, 2 * HD), bf16),
            pltpu.VMEM((2, 2, 2, rows, HD), bf16),
            pltpu.VMEM((QUAD, 8, LINE), jnp.int32),
            pltpu.VMEM((rows, WIDE), bf16),
            pltpu.VMEM(docs.shape, jnp.int32),
            pltpu.VMEM(docs.shape, jnp.int32),
            dma((8,)),
            dma((3, parts)),
            dma((3, parts)),
            dma((3,)),
            dma((3,)),
            dma((3,)),
            dma((3,)),
            dma((2, fsdp, 2)),
            dma((2, fsdp + 1, 2)),
            dma((2, fsdp, 2)),
            dma((2, fsdp, 2)),
            dma((2, 2, fsdp)),
            dma((2, 2, fsdp + 1)),
            dma((2, 2 * fsdp, 2)),
            dma((2, 2 * fsdp, 2)),
            dma((2,)),
        ],
        compiler_params=pltpu.CompilerParams(
            collective_id=0, has_side_effects=True, vmem_limit_bytes=32 * 1024 * 1024
        ),
        name="gather",
    )(marked, docs, *(pltpu.with_memory_space_constraint(x, pltpu.HBM) for x in (hidden, kv_weights, queries)))


def attend_kernel(key_block, slot, limits_ref, q_ref, k_ref, after_ref, out_ref, qt, top, total, acc):
    rows = q_ref.shape[1]
    lo_ref = limits_ref.at[slot : slot + 1]
    hi_ref = limits_ref.at[QUAD + slot : QUAD + slot + 1]
    lo, hi = lo_ref[...], hi_ref[...]
    lo_min, lo_max, hi_min, hi_max = jnp.min(lo), jnp.max(lo), jnp.min(hi), jnp.max(hi)
    first = lax.div(lo_min, key_block)
    end = lax.div(hi_max, key_block) + 1
    full_first = jnp.minimum(lax.div(lo_max + key_block - 1, key_block), end)
    full_end = jnp.maximum(lax.div(hi_min + 1, key_block), full_first)

    lanes = [slice(g * rows, (g + 1) * rows) for g in range(PER)]
    factor = math.log2(math.e) / math.sqrt(HD)
    for g in range(PER):
        qt[:, g * rows : (g + 1) * rows] = q_ref[slot, :, g * HD : (g + 1) * HD].T
    top[...] = jnp.full_like(top, NEG)
    total[...] = jnp.zeros_like(total)
    acc[...] = jnp.zeros_like(acc)

    def step(masked, b, _):
        at = pl.multiple_of(b * key_block, key_block)
        keys = k_ref[0, pl.ds(at, key_block), :]
        values = k_ref[1, pl.ds(at, key_block), :]
        if masked:
            place = at + lax.broadcasted_iota(jnp.int32, (key_block, rows), 0)
            allowed = jnp.logical_and(place >= lo_ref[...], place <= hi_ref[...])
        scores = [jnp.dot(keys, qt[:, at_g], preferred_element_type=jnp.float32) for at_g in lanes]
        if masked:
            scores = [jnp.where(allowed, score, NEG) for score in scores]
        before = [top[:, at_g] for at_g in lanes]
        peak = [
            jnp.maximum(old, jnp.max(score, axis=0, keepdims=True))
            for old, score in zip(before, scores)
        ]
        weights = [jnp.exp2((score - high) * factor) for score, high in zip(scores, peak)]
        shrink = [jnp.exp2((old - high) * factor) for old, high in zip(before, peak)]
        added = [jnp.sum(weight, axis=0, keepdims=True) for weight in weights]
        mixed = [
            lax.dot_general(
                values,
                weight.astype(jnp.bfloat16),
                (((0,), (0,)), ((), ())),
                preferred_element_type=jnp.float32,
            )
            for weight in weights
        ]
        for g, at_g in enumerate(lanes):
            top[:, at_g] = peak[g]
            total[:, at_g] = total[:, at_g] * shrink[g] + added[g]
            acc[:, at_g] = acc[:, at_g] * shrink[g] + mixed[g]
        return 0

    lax.fori_loop(first, full_first, functools.partial(step, True), 0)
    lax.fori_loop(full_first, full_end, functools.partial(step, False), 0)
    lax.fori_loop(full_end, end, functools.partial(step, True), 0)
    for g in range(PER):
        mixed = (acc[:, lanes[g]] / total[:, lanes[g]]).T
        out_ref[:, g * HD : (g + 1) * HD] = mixed.astype(out_ref.dtype)


def attend(kv, queries, limits, after, slot):
    fsdp = lax.axis_size("fsdp")
    _, rows, wide = queries.shape
    n_keys = kv.shape[1] * kv.shape[2] * kv.shape[3]
    kv = kv.reshape(2, n_keys, HD)
    key_block = math.gcd(rows * fsdp, 512)
    vmem = pl.BlockSpec(memory_space=pltpu.VMEM)
    work = rows * PER * n_keys // 4
    return pl.pallas_call(
        functools.partial(attend_kernel, key_block, slot),
        in_specs=[vmem] * 3 + [pl.BlockSpec(memory_space=pl.ANY)],
        out_specs=vmem,
        out_shape=jax.ShapeDtypeStruct((rows, wide), queries.dtype),
        scratch_shapes=[
            pltpu.VMEM((HD, PER * rows), jnp.bfloat16),
            pltpu.VMEM((1, PER * rows), jnp.float32),
            pltpu.VMEM((1, PER * rows), jnp.float32),
            pltpu.VMEM((HD, PER * rows), jnp.float32),
        ],
        compiler_params=pltpu.CompilerParams(vmem_limit_bytes=16 * 1024 * 1024),
        cost_estimate=pl.CostEstimate(flops=4 * HD * work, bytes_accessed=4 * HD * n_keys, transcendentals=work),
    )(limits, queries, kv, after)


def assemble_kernel(*refs):
    h = lax.axis_index("seq") % QUAD
    out_ref, sems = refs[QUAD:]
    wide = refs[0].shape[1]
    copies = [
        pltpu.make_async_copy(
            refs[slot], out_ref.at[:, pl.ds(pl.multiple_of(flip(h, slot) * wide, HD), wide)], sems.at[slot]
        )
        for slot in range(QUAD)
    ]
    for copy in copies:
        copy.start()
    for copy in copies:
        copy.wait()


def assemble(pieces):
    rows, wide = pieces[0].shape
    return pl.pallas_call(
        assemble_kernel,
        in_specs=[pl.BlockSpec(memory_space=pltpu.VMEM)] * QUAD,
        out_specs=pl.BlockSpec(memory_space=pl.ANY),
        out_shape=jax.ShapeDtypeStruct((rows, QUAD * wide), pieces[0].dtype),
        scratch_shapes=[pltpu.SemaphoreType.DMA((QUAD,))],
        compiler_params=pltpu.CompilerParams(vmem_limit_bytes=8 * 1024 * 1024),
        name="assemble",
    )(*pieces)


def local(hidden, queries, kv_weights, image_groups, doc_ids):
    seq = lax.axis_size("seq")
    kv, q, limits = gather(hidden, queries, kv_weights, image_groups, doc_ids)
    pieces = [None] * QUAD
    mixed = limits
    for slot in (3, 2, 1, 0):
        mixed = attend(kv, q, limits, mixed, slot)
        swap = [(i, i ^ slot) for i in range(seq)]
        pieces[slot] = lax.ppermute(mixed, "seq", swap) if slot else mixed
    return assemble(pieces)


def solution(mesh):
    in_specs = (
        P(("seq", "fsdp"), None),
        P(("seq", "fsdp"), None),
        P(None, "fsdp", None),
        P("seq"),
        P(),
    )
    out_specs = P(("seq", "fsdp"), None)
    return jax.shard_map(local, mesh=mesh, in_specs=in_specs, out_specs=out_specs, check_vma=False)
```

```python
import functools
import math

import jax
import jax.numpy as jnp
from jax import lax
from jax.experimental import pallas as pl
from jax.experimental.pallas import tpu as pltpu
from jax.sharding import PartitionSpec as P


KVH = 4
HD = 128
QH = 16
SPAN = 3
NEG = -1e30
QUAD = KVH
PER = QH // KVH
WIDE = PER * HD
LINE = 128
MESH = pl.DeviceIdType.MESH


def flip(place, bits):
    out = place
    bit = 1
    while bit <= bits:
        if bits & bit:
            out = out + bit * (1 - 2 * (lax.div(place, bit) % 2))
        bit *= 2
    return out


def gather_kernel(
    seq, fsdp, parts, mod_ref, docs_ref, hidden_ref, w_ref, q_ref,
    kv_out, q_out, limits,
    hid, w, made, mods, q_own, docs, starts, ends,
    local, hid_send, hid_recv, mod_send, mod_recv, q_send, q_recv,
    wz_send, wz_recv, wy_send, wy_recv, kz_send, kz_recv, ky_send, ky_recv, made_sem,
):
    s = lax.axis_index("seq")
    z = lax.axis_index("fsdp")
    h = s % QUAD
    carried = lax.div(s, QUAD) % 2
    base = s - h
    twin, across, diag, partner = flip(s, 1), flip(s, 2), flip(s, 3), flip(s, 4)
    ahead, behind = s + QUAD, s - QUAD
    has_ahead, has_behind = ahead < seq, behind >= 0
    step = hidden_ref.shape[0] // parts
    depth = w_ref.shape[1]
    lines = [(way, d) for d in range(1, fsdp) for way in (0, 1)]

    def exists(way, d):
        return z - d >= 0 if way == 0 else z + d <= fsdp - 1

    def source(way, d):
        return z - d if way == 0 else z + d

    def goes_on(way):
        return z + 1 <= fsdp - 1 if way == 0 else z >= 1

    def onward(way):
        return (s, z + 1) if way == 0 else (s, z - 1)

    def columns(head, half):
        return pl.ds(pl.multiple_of((half * KVH + head) * HD, HD), HD)

    def remote(src, dst, send, recv, device):
        return pltpu.make_async_remote_copy(
            src_ref=src, dst_ref=dst, send_sem=send, recv_sem=recv, device_id=device, device_id_type=MESH
        )

    keep = [pltpu.make_async_copy(hidden_ref, hid.at[h], local.at[0])]
    for m in range(2):
        for half in range(2):
            keep.append(
                pltpu.make_async_copy(
                    w_ref.at[m, :, columns(h, half)],
                    w.at[z, m, :, half * HD : (half + 1) * HD],
                    local.at[1 + 2 * m + half],
                )
            )
    q_in = pltpu.make_async_copy(q_ref.at[:, pl.ds(pl.multiple_of(h * WIDE, HD), WIDE)], q_own, local.at[5])
    q_keep = pltpu.make_async_copy(q_own, q_out.at[0], local.at[6])
    mod_in = pltpu.make_async_copy(mod_ref, mods.at[h], local.at[7])
    docs_in = pltpu.make_async_copy(docs_ref, docs, local.at[8])
    docs_in.start()
    for copy in keep:
        copy.start()
    q_in.start()
    mod_in.start()

    barrier = pltpu.get_barrier_semaphore()
    near = [(twin, z), (across, z), (diag, z), (partner, z)]
    near += [((s + QUAD) % seq, z), ((s - QUAD + seq) % seq, z)]
    for device in near:
        pl.semaphore_signal(barrier, inc=1, device_id=device, device_id_type=MESH)
    for way in (0, 1):
        @pl.when(goes_on(way))
        def _(way=way):
            pl.semaphore_signal(barrier, inc=1, device_id=onward(way), device_id_type=MESH)
    both = (z >= 1).astype(jnp.int32) + (z <= fsdp - 2).astype(jnp.int32)
    pl.semaphore_wait(barrier, len(near) + both)

    def w_slot(zs, m, half):
        return w.at[zs, m, :, half * HD : (half + 1) * HD]

    def w_line(way, d, half):
        src = w_ref.at[carried, :, columns(h, half)] if d == 0 else w_slot(source(way, d), carried, half)
        zs = z if d == 0 else source(way, d)
        return remote(
            src, w_slot(zs, carried, half), wz_send.at[way, d, half], wz_recv.at[way, d + 1, half], onward(way)
        )

    def w_arrived(way, d, half):
        return remote(
            w_slot(source(way, d), carried, half), w_slot(source(way, d), carried, half),
            wz_send.at[way, d, half], wz_recv.at[way, d, half], (s, z),
        )

    def w_swap(way, d, half):
        slot = w_slot(source(way, d), carried, half)
        return remote(slot, slot, wy_send.at[way, d, half], wy_recv.at[way, d, half], (partner, z))

    def w_swapped(way, d, half):
        slot = w_slot(source(way, d), 1 - carried, half)
        return remote(slot, slot, wy_send.at[way, d, half], wy_recv.at[way, d, half], (partner, z))

    def rows(part):
        return slice(part * step, (part + 1) * step)

    def hid_to(which, device, part):
        return remote(
            hidden_ref.at[rows(part)], hid.at[h, rows(part)],
            hid_send.at[which, part], hid_recv.at[which, part], (device, z),
        )

    def hid_relay(part):
        slot = hid.at[across - base, rows(part)]
        return remote(slot, slot, hid_send.at[2, part], hid_recv.at[2, part], (twin, z))

    def hid_got(which, device, part):
        slot = hid.at[device - base, rows(part)]
        return remote(slot, slot, hid_send.at[which, part], hid_recv.at[which, part], (twin, z))

    mates = (twin, across, diag)

    def mod_to(i):
        return remote(mod_ref, mods.at[h], mod_send.at[i], mod_recv.at[i], (mates[i], z))

    def mod_got(i):
        slot = mods.at[mates[i] - base]
        return remote(slot, slot, mod_send.at[i], mod_recv.at[i], (mates[i], z))

    def q_to(i):
        head = mates[i] - base
        return remote(
            q_ref.at[:, pl.ds(pl.multiple_of(head * WIDE, HD), WIDE)], q_out.at[1 + i],
            q_send.at[i], q_recv.at[i], (mates[i], z),
        )

    def q_got(i):
        slot = q_out.at[1 + i]
        return remote(slot, slot, q_send.at[i], q_recv.at[i], (mates[i], z))

    groups = [flip(s, unit) - base for unit in range(QUAD)]

    def kv_slot(unit, zs):
        return kv_out.at[:, SPAN + groups[unit], zs]

    def kv_line(unit, way, d):
        src = made.at[unit] if d == 0 else kv_slot(unit, source(way, d))
        zs = z if d == 0 else source(way, d)
        return remote(
            src, kv_slot(unit, zs), kz_send.at[unit, way, d], kz_recv.at[unit, way, d + 1], onward(way)
        )

    def kv_arrived(unit, way, d):
        slot = kv_slot(unit, source(way, d))
        return remote(slot, slot, kz_send.at[unit, way, d], kz_recv.at[unit, way, d], (s, z))

    def ahead_index(way, d):
        return 0 if d == 0 else 1 + 2 * (d - 1) + way

    def kv_ahead(unit, way, d):
        zs = z if d == 0 else source(way, d)
        src = made.at[unit] if d == 0 else kv_slot(unit, zs)
        at = ahead_index(way, d)
        return remote(
            src, kv_out.at[:, groups[unit] - 1, zs], ky_send.at[unit, at], ky_recv.at[unit, at], (ahead, z)
        )

    def kv_behind(unit, way, d):
        zs = z if d == 0 else source(way, d)
        slot = kv_out.at[:, groups[unit] - 1, zs]
        at = ahead_index(way, d)
        return remote(slot, slot, ky_send.at[unit, at], ky_recv.at[unit, at], (ahead, z))

    def kv_keep(unit):
        return pltpu.make_async_copy(made.at[unit], kv_slot(unit, z), made_sem.at[unit])

    def when(holds, act):
        @pl.when(holds)
        def _():
            act()

    for half in range(2):
        for way in (0, 1):
            when(goes_on(way), lambda: w_line(way, 0, half).start())
    for i in range(3):
        mod_to(i).start()
    for part in range(parts):
        hid_to(1, across, part).start()
    for part in range(parts):
        hid_to(0, twin, part).start()
    for i in (1, 2, 0):
        q_to(i).start()

    def pass_weights(way, d, half):
        def act():
            w_arrived(way, d, half).wait_recv()
            if d < fsdp - 1:
                when(goes_on(way), lambda: w_line(way, d, half).start())
            w_swap(way, d, half).start()

        when(exists(way, d), act)

    def pass_hidden(part):
        hid_got(1, across, part).wait_recv()
        hid_relay(part).start()

    def send_ahead(unit, way, d):
        when(jnp.logical_and(has_ahead, groups[unit] >= 1), lambda: kv_ahead(unit, way, d).start())

    def pass_kv(unit, way, d):
        def act():
            kv_arrived(unit, way, d).wait_recv()
            if d < fsdp - 1:
                when(goes_on(way), lambda: kv_line(unit, way, d).start())
            send_ahead(unit, way, d)

        when(exists(way, d), act)

    def project(unit):
        group = groups[unit]
        image = jnp.max(mods[group]) == 1
        total = None
        for zs in range(fsdp):
            weight = jnp.where(image, w[zs, 1], w[zs, 0])
            rows_at = hid[group, :, zs * depth : (zs + 1) * depth]
            term = jnp.dot(rows_at, weight, preferred_element_type=jnp.float32)
            total = term if total is None else total + term
        rounded = total.astype(jnp.bfloat16)
        made[unit, 0] = rounded[:, :HD]
        made[unit, 1] = rounded[:, HD:]

    def send_made(unit):
        for way in (0, 1):
            when(goes_on(way), lambda: kv_line(unit, way, 0).start())
        send_ahead(unit, 0, 0)
        kv_keep(unit).start()

    docs_in.wait()
    starts[...], ends[...] = bounds(docs[...])
    mod_in.wait()
    for i in range(3):
        mod_got(i).wait_recv()
    block = hidden_ref.shape[0] * fsdp
    origin = (base - SPAN) * block
    for slot in range(QUAD):
        group = flip(s, slot)
        image = mods[group - base, :1] == 1
        for i in range(hidden_ref.shape[0] // LINE):
            first = group * block + z * hidden_ref.shape[0] + i * LINE
            line = lax.div(first, LINE)
            at = slice(i * LINE, (i + 1) * LINE)
            place = first + lax.broadcasted_iota(jnp.int32, (1, LINE), 1)
            last = jnp.minimum(ends[pl.ds(line, 1), :], group * block + block - 1)
            limits[slot : slot + 1, at] = starts[pl.ds(line, 1), :] - origin
            limits[QUAD + slot : QUAD + slot + 1, at] = jnp.where(image, last, place) - origin

    done = 0
    for d in range(1, fsdp):
        for half in range(2):
            for way in (0, 1):
                pass_weights(way, d, half)
        if done < parts - 2:
            pass_hidden(done)
            done += 1
    for copy in keep:
        copy.wait()
    for part in range(parts):
        hid_got(0, twin, part).wait_recv()
    for way, d in lines:
        for half in range(2):
            when(exists(way, d), lambda: w_swapped(way, d, half).wait_recv())
    project(0)
    q_in.wait()
    q_keep.start()
    project(1)
    send_made(0)
    send_made(1)

    def relay(unit, d):
        for way in (0, 1):
            pass_kv(unit, way, d)

    pass_hidden(parts - 2)
    relay(0, 1)
    relay(1, 1)
    pass_hidden(parts - 1)
    relay(0, 2)
    for part in range(parts):
        hid_got(2, diag, part).wait_recv()
    project(2)
    relay(1, 2)
    project(3)
    send_made(2)
    send_made(3)
    for d in range(3, fsdp):
        relay(0, d)
        relay(1, d)
    for d in range(1, fsdp):
        relay(2, d)
        relay(3, d)
    for i in range(3):
        q_got(i).wait_recv()
    for unit in range(QUAD):
        for way, d in [(0, 0)] + lines:
            holds = jnp.logical_and(has_behind, groups[unit] >= 1)
            if d:
                holds = jnp.logical_and(holds, exists(way, d))
            when(holds, lambda: kv_behind(unit, way, d).wait_recv())

    q_keep.wait()
    for unit in range(QUAD):
        kv_keep(unit).wait()
    for half in range(2):
        for way in (0, 1):
            when(goes_on(way), lambda: w_line(way, 0, half).wait_send())
            for d in range(1, fsdp):
                def act(way=way, d=d, half=half):
                    if d < fsdp - 1:
                        when(goes_on(way), lambda: w_line(way, d, half).wait_send())
                    w_swap(way, d, half).wait_send()

                when(exists(way, d), act)
    for i in range(3):
        mod_to(i).wait_send()
        q_to(i).wait_send()
    for part in range(parts):
        hid_to(0, twin, part).wait_send()
        hid_to(1, across, part).wait_send()
        hid_relay(part).wait_send()

    def sent_ahead(unit, way, d):
        when(jnp.logical_and(has_ahead, groups[unit] >= 1), lambda: kv_ahead(unit, way, d).wait_send())

    for unit in range(QUAD):
        for way in (0, 1):
            when(goes_on(way), lambda: kv_line(unit, way, 0).wait_send())
        sent_ahead(unit, 0, 0)
        for way, d in lines:
            def act(unit=unit, way=way, d=d):
                if d < fsdp - 1:
                    when(goes_on(way), lambda: kv_line(unit, way, d).wait_send())
                sent_ahead(unit, way, d)

            when(exists(way, d), act)


def shifted(x, by, axis, fill):
    size = x.shape[axis]
    place = lax.broadcasted_iota(jnp.int32, x.shape, axis)
    moved = pltpu.roll(x, by % size, axis)
    inside = place >= by if by > 0 else place < size + by
    return jnp.where(inside, moved, fill)


def spread(x, pick, sign, fill):
    by = 1
    while by < x.shape[1]:
        x = pick(x, shifted(x, sign * by, 1, fill))
        by *= 2
    edge = x[:, -1:] if sign > 0 else x[:, :1]
    rows = shifted(jnp.broadcast_to(edge, x.shape), sign, 0, fill)
    by = 1
    while by < x.shape[0]:
        rows = pick(rows, shifted(rows, sign * by, 0, fill))
        by *= 2
    return pick(x, rows)


def bounds(docs):
    count = docs.shape[0] * docs.shape[1]
    place = (
        lax.broadcasted_iota(jnp.int32, docs.shape, 0) * docs.shape[1]
        + lax.broadcasted_iota(jnp.int32, docs.shape, 1)
    )
    lane = lax.broadcasted_iota(jnp.int32, docs.shape, 1)
    width = docs.shape[1]
    turned = pltpu.roll(docs, 1, 1)
    before = jnp.where(lane == 0, shifted(turned, 1, 0, -1), turned)
    turned = pltpu.roll(docs, width - 1, 1)
    after = jnp.where(lane == width - 1, shifted(turned, -1, 0, -1), turned)
    starts = jnp.where(docs != before, place, 0)
    ends = jnp.where(docs != after, place, count - 1)
    return spread(starts, jnp.maximum, 1, 0), spread(ends, jnp.minimum, -1, count - 1)


def gather(hidden, queries, kv_weights, image_groups, doc_ids):
    seq, fsdp = lax.axis_size("seq"), lax.axis_size("fsdp")
    rows, width = hidden.shape
    depth = kv_weights.shape[1]
    parts = 4
    marked = jnp.broadcast_to(image_groups[0], (8, LINE))
    docs = doc_ids.reshape(-1, LINE)
    anywhere = pl.BlockSpec(memory_space=pl.ANY)
    far = pl.BlockSpec(memory_space=pltpu.HBM)
    vmem = pl.BlockSpec(memory_space=pltpu.VMEM)
    dma = pltpu.SemaphoreType.DMA
    bf16 = jnp.bfloat16
    return pl.pallas_call(
        functools.partial(gather_kernel, seq, fsdp, parts),
        in_specs=[far] * 5,
        out_specs=[anywhere, anywhere, vmem],
        out_shape=[
            jax.ShapeDtypeStruct((2, SPAN + QUAD, fsdp, rows, HD), bf16),
            jax.ShapeDtypeStruct((QUAD, rows, WIDE), bf16),
            jax.ShapeDtypeStruct((2 * QUAD, rows), jnp.int32),
        ],
        scratch_shapes=[
            pltpu.VMEM((QUAD, rows, width), bf16),
            pltpu.VMEM((fsdp, 2, depth, 2 * HD), bf16),
            pltpu.VMEM((QUAD, 2, rows, HD), bf16),
            pltpu.VMEM((QUAD, 8, LINE), jnp.int32),
            pltpu.VMEM((rows, WIDE), bf16),
            pltpu.VMEM(docs.shape, jnp.int32),
            pltpu.VMEM(docs.shape, jnp.int32),
            pltpu.VMEM(docs.shape, jnp.int32),
            dma((9,)),
            dma((3, parts)),
            dma((3, parts)),
            dma((3,)),
            dma((3,)),
            dma((3,)),
            dma((3,)),
            dma((2, fsdp, 2)),
            dma((2, fsdp + 1, 2)),
            dma((2, fsdp, 2)),
            dma((2, fsdp, 2)),
            dma((QUAD, 2, fsdp)),
            dma((QUAD, 2, fsdp + 1)),
            dma((QUAD, 2 * fsdp)),
            dma((QUAD, 2 * fsdp)),
            dma((QUAD,)),
        ],
        compiler_params=pltpu.CompilerParams(
            collective_id=0, has_side_effects=True, vmem_limit_bytes=32 * 1024 * 1024
        ),
        name="gather",
    )(marked, *(pltpu.with_memory_space_constraint(x, pltpu.HBM) for x in (docs, hidden, kv_weights, queries)))


def attend_kernel(key_block, slot, limits_ref, q_ref, k_ref, after_ref, out_ref, qt, top, total, acc):
    rows = q_ref.shape[1]
    lo_ref = limits_ref.at[slot : slot + 1]
    hi_ref = limits_ref.at[QUAD + slot : QUAD + slot + 1]
    lo, hi = lo_ref[...], hi_ref[...]
    lo_min, lo_max, hi_min, hi_max = jnp.min(lo), jnp.max(lo), jnp.min(hi), jnp.max(hi)
    first = lax.div(lo_min, key_block)
    end = lax.div(hi_max, key_block) + 1
    full_first = jnp.minimum(lax.div(lo_max + key_block - 1, key_block), end)
    full_end = jnp.maximum(lax.div(hi_min + 1, key_block), full_first)

    lanes = [slice(g * rows, (g + 1) * rows) for g in range(PER)]
    factor = math.log2(math.e) / math.sqrt(HD)
    for g in range(PER):
        qt[:, g * rows : (g + 1) * rows] = q_ref[slot, :, g * HD : (g + 1) * HD].T
    top[...] = jnp.full_like(top, NEG)
    total[...] = jnp.zeros_like(total)
    acc[...] = jnp.zeros_like(acc)

    def step(masked, b, _):
        at = pl.multiple_of(b * key_block, key_block)
        keys = k_ref[0, pl.ds(at, key_block), :]
        values = k_ref[1, pl.ds(at, key_block), :]
        if masked:
            place = at + lax.broadcasted_iota(jnp.int32, (key_block, rows), 0)
            allowed = jnp.logical_and(place >= lo_ref[...], place <= hi_ref[...])
        scores = [jnp.dot(keys, qt[:, at_g], preferred_element_type=jnp.float32) for at_g in lanes]
        if masked:
            scores = [jnp.where(allowed, score, NEG) for score in scores]
        before = [top[:, at_g] for at_g in lanes]
        peak = [
            jnp.maximum(old, jnp.max(score, axis=0, keepdims=True))
            for old, score in zip(before, scores)
        ]
        weights = [jnp.exp2((score - high) * factor) for score, high in zip(scores, peak)]
        shrink = [jnp.exp2((old - high) * factor) for old, high in zip(before, peak)]
        added = [jnp.sum(weight, axis=0, keepdims=True) for weight in weights]
        mixed = [
            lax.dot_general(
                values,
                weight.astype(jnp.bfloat16),
                (((0,), (0,)), ((), ())),
                preferred_element_type=jnp.float32,
            )
            for weight in weights
        ]
        for g, at_g in enumerate(lanes):
            top[:, at_g] = peak[g]
            total[:, at_g] = total[:, at_g] * shrink[g] + added[g]
            acc[:, at_g] = acc[:, at_g] * shrink[g] + mixed[g]
        return 0

    lax.fori_loop(first, full_first, functools.partial(step, True), 0)
    lax.fori_loop(full_first, full_end, functools.partial(step, False), 0)
    lax.fori_loop(full_end, end, functools.partial(step, True), 0)
    for g in range(PER):
        mixed = (acc[:, lanes[g]] / total[:, lanes[g]]).T
        out_ref[:, g * HD : (g + 1) * HD] = mixed.astype(out_ref.dtype)


def attend(kv, queries, limits, after, slot):
    fsdp = lax.axis_size("fsdp")
    _, rows, wide = queries.shape
    n_keys = kv.shape[1] * kv.shape[2] * kv.shape[3]
    kv = kv.reshape(2, n_keys, HD)
    key_block = math.gcd(rows * fsdp, 512)
    vmem = pl.BlockSpec(memory_space=pltpu.VMEM)
    work = rows * PER * n_keys // 4
    return pl.pallas_call(
        functools.partial(attend_kernel, key_block, slot),
        in_specs=[vmem] * 3 + [pl.BlockSpec(memory_space=pl.ANY)],
        out_specs=vmem,
        out_shape=jax.ShapeDtypeStruct((rows, wide), queries.dtype),
        scratch_shapes=[
            pltpu.VMEM((HD, PER * rows), jnp.bfloat16),
            pltpu.VMEM((1, PER * rows), jnp.float32),
            pltpu.VMEM((1, PER * rows), jnp.float32),
            pltpu.VMEM((HD, PER * rows), jnp.float32),
        ],
        compiler_params=pltpu.CompilerParams(vmem_limit_bytes=16 * 1024 * 1024),
        cost_estimate=pl.CostEstimate(flops=4 * HD * work, bytes_accessed=4 * HD * n_keys, transcendentals=work),
    )(limits, queries, kv, after)


def assemble_kernel(*refs):
    h = lax.axis_index("seq") % QUAD
    out_ref, sems = refs[QUAD:]
    wide = refs[0].shape[1]
    copies = [
        pltpu.make_async_copy(
            refs[slot], out_ref.at[:, pl.ds(pl.multiple_of(flip(h, slot) * wide, HD), wide)], sems.at[slot]
        )
        for slot in range(QUAD)
    ]
    for copy in copies:
        copy.start()
    for copy in copies:
        copy.wait()


def assemble(pieces):
    rows, wide = pieces[0].shape
    return pl.pallas_call(
        assemble_kernel,
        in_specs=[pl.BlockSpec(memory_space=pltpu.VMEM)] * QUAD,
        out_specs=pl.BlockSpec(memory_space=pl.ANY),
        out_shape=jax.ShapeDtypeStruct((rows, QUAD * wide), pieces[0].dtype),
        scratch_shapes=[pltpu.SemaphoreType.DMA((QUAD,))],
        compiler_params=pltpu.CompilerParams(vmem_limit_bytes=8 * 1024 * 1024),
        name="assemble",
    )(*pieces)


def local(hidden, queries, kv_weights, image_groups, doc_ids):
    seq = lax.axis_size("seq")
    kv, q, limits = gather(hidden, queries, kv_weights, image_groups, doc_ids)
    pieces = [None] * QUAD
    mixed = limits
    for slot in (3, 2, 1, 0):
        mixed = attend(kv, q, limits, mixed, slot)
        swap = [(i, i ^ slot) for i in range(seq)]
        pieces[slot] = lax.ppermute(mixed, "seq", swap) if slot else mixed
    return assemble(pieces)


def solution(mesh):
    in_specs = (
        P(("seq", "fsdp"), None),
        P(("seq", "fsdp"), None),
        P(None, "fsdp", None),
        P("seq"),
        P(),
    )
    out_specs = P(("seq", "fsdp"), None)
    return jax.shard_map(local, mesh=mesh, in_specs=in_specs, out_specs=out_specs, check_vma=False)
```

```python
import functools
import math

import jax
import jax.numpy as jnp
from jax import lax
from jax.experimental import pallas as pl
from jax.experimental.pallas import tpu as pltpu
from jax.sharding import PartitionSpec as P


KVH = 4
HD = 128
QH = 16
SPAN = 3
NEG = -1e30
QUAD = KVH
PER = QH // KVH
WIDE = PER * HD
LINE = 128
MESH = pl.DeviceIdType.MESH


def flip(place, bits):
    out = place
    bit = 1
    while bit <= bits:
        if bits & bit:
            out = out + bit * (1 - 2 * (lax.div(place, bit) % 2))
        bit *= 2
    return out


def gather_kernel(
    seq, fsdp, parts, mod_ref, docs_ref, hidden_ref, w_ref, q_ref,
    kv_out, q_out, limits,
    hid, w, made, mods, q_own, docs, starts, ends,
    local, hid_send, hid_recv, mod_send, mod_recv, q_send, q_recv,
    wz_send, wz_recv, wy_send, wy_recv, kz_send, kz_recv, ky_send, ky_recv, made_sem,
):
    s = lax.axis_index("seq")
    z = lax.axis_index("fsdp")
    h = s % QUAD
    carried = lax.div(s, QUAD) % 2
    base = s - h
    twin, across, diag, partner = flip(s, 1), flip(s, 2), flip(s, 3), flip(s, 4)
    ahead, behind = s + QUAD, s - QUAD
    has_ahead, has_behind = ahead < seq, behind >= 0
    step = hidden_ref.shape[0] // parts
    depth = w_ref.shape[1]
    lines = [(way, d) for d in range(1, fsdp) for way in (0, 1)]

    def exists(way, d):
        return z - d >= 0 if way == 0 else z + d <= fsdp - 1

    def source(way, d):
        return z - d if way == 0 else z + d

    def goes_on(way):
        return z + 1 <= fsdp - 1 if way == 0 else z >= 1

    def onward(way):
        return (s, z + 1) if way == 0 else (s, z - 1)

    def columns(head, half):
        return pl.ds(pl.multiple_of((half * KVH + head) * HD, HD), HD)

    def remote(src, dst, send, recv, device):
        return pltpu.make_async_remote_copy(
            src_ref=src, dst_ref=dst, send_sem=send, recv_sem=recv, device_id=device, device_id_type=MESH
        )

    keep = [pltpu.make_async_copy(hidden_ref, hid.at[h], local.at[0])]
    for m in range(2):
        for half in range(2):
            keep.append(
                pltpu.make_async_copy(
                    w_ref.at[m, :, columns(h, half)],
                    w.at[z, m, half],
                    local.at[1 + 2 * m + half],
                )
            )
    q_in = pltpu.make_async_copy(q_ref.at[:, pl.ds(pl.multiple_of(h * WIDE, HD), WIDE)], q_own, local.at[5])
    q_keep = pltpu.make_async_copy(q_own, q_out.at[0], local.at[6])
    mod_in = pltpu.make_async_copy(mod_ref, mods.at[h], local.at[7])
    docs_in = pltpu.make_async_copy(docs_ref, docs, local.at[8])
    docs_in.start()
    for copy in keep:
        copy.start()
    q_in.start()
    mod_in.start()

    barrier = pltpu.get_barrier_semaphore()
    near = [(twin, z), (across, z), (diag, z), (partner, z)]
    near += [((s + QUAD) % seq, z), ((s - QUAD + seq) % seq, z)]
    for device in near:
        pl.semaphore_signal(barrier, inc=1, device_id=device, device_id_type=MESH)
    for way in (0, 1):
        @pl.when(goes_on(way))
        def _(way=way):
            pl.semaphore_signal(barrier, inc=1, device_id=onward(way), device_id_type=MESH)
    both = (z >= 1).astype(jnp.int32) + (z <= fsdp - 2).astype(jnp.int32)
    pl.semaphore_wait(barrier, len(near) + both)

    def w_slot(zs, m, half):
        return w.at[zs, m, half]

    def w_line(way, d, half):
        zs = z if d == 0 else source(way, d)
        return remote(
            w_slot(zs, carried, half), w_slot(zs, carried, half), wz_send.at[way, d, half], wz_recv.at[way, d + 1, half], onward(way)
        )

    def w_arrived(way, d, half):
        return remote(
            w_slot(source(way, d), carried, half), w_slot(source(way, d), carried, half),
            wz_send.at[way, d, half], wz_recv.at[way, d, half], (s, z),
        )

    def w_swap(way, d, half):
        slot = w_slot(source(way, d), carried, half)
        return remote(slot, slot, wy_send.at[way, d, half], wy_recv.at[way, d, half], (partner, z))

    def w_swapped(way, d, half):
        slot = w_slot(source(way, d), 1 - carried, half)
        return remote(slot, slot, wy_send.at[way, d, half], wy_recv.at[way, d, half], (partner, z))

    def rows(part):
        return slice(part * step, (part + 1) * step)

    def hid_to(which, device, part):
        return remote(
            hidden_ref.at[rows(part)], hid.at[h, rows(part)],
            hid_send.at[which, part], hid_recv.at[which, part], (device, z),
        )

    def hid_relay(part):
        slot = hid.at[across - base, rows(part)]
        return remote(slot, slot, hid_send.at[2, part], hid_recv.at[2, part], (twin, z))

    def hid_got(which, device, part):
        slot = hid.at[device - base, rows(part)]
        return remote(slot, slot, hid_send.at[which, part], hid_recv.at[which, part], (twin, z))

    mates = (twin, across, diag)

    def mod_to(i):
        return remote(mod_ref, mods.at[h], mod_send.at[i], mod_recv.at[i], (mates[i], z))

    def mod_got(i):
        slot = mods.at[mates[i] - base]
        return remote(slot, slot, mod_send.at[i], mod_recv.at[i], (mates[i], z))

    def q_to(i):
        head = mates[i] - base
        return remote(
            q_ref.at[:, pl.ds(pl.multiple_of(head * WIDE, HD), WIDE)], q_out.at[1 + i],
            q_send.at[i], q_recv.at[i], (mates[i], z),
        )

    def q_got(i):
        slot = q_out.at[1 + i]
        return remote(slot, slot, q_send.at[i], q_recv.at[i], (mates[i], z))

    side = lax.div(h, 2)
    groups = [2 * side + 1, 2 * side, 3 - 2 * side, 2 - 2 * side]

    def kv_slot(unit, zs):
        return kv_out.at[:, SPAN + groups[unit], zs]

    def kv_line(unit, way, d):
        src = made.at[unit] if d == 0 else kv_slot(unit, source(way, d))
        zs = z if d == 0 else source(way, d)
        return remote(
            src, kv_slot(unit, zs), kz_send.at[unit, way, d], kz_recv.at[unit, way, d + 1], onward(way)
        )

    def kv_arrived(unit, way, d):
        slot = kv_slot(unit, source(way, d))
        return remote(slot, slot, kz_send.at[unit, way, d], kz_recv.at[unit, way, d], (s, z))

    def ahead_index(way, d):
        return 0 if d == 0 else 1 + 2 * (d - 1) + way

    def kv_ahead(unit, way, d):
        zs = z if d == 0 else source(way, d)
        src = made.at[unit] if d == 0 else kv_slot(unit, zs)
        at = ahead_index(way, d)
        return remote(
            src, kv_out.at[:, groups[unit] - 1, zs], ky_send.at[unit, at], ky_recv.at[unit, at], (ahead, z)
        )

    def kv_behind(unit, way, d):
        zs = z if d == 0 else source(way, d)
        slot = kv_out.at[:, groups[unit] - 1, zs]
        at = ahead_index(way, d)
        return remote(slot, slot, ky_send.at[unit, at], ky_recv.at[unit, at], (ahead, z))

    def kv_keep(unit):
        return pltpu.make_async_copy(made.at[unit], kv_slot(unit, z), made_sem.at[unit])

    def when(holds, act):
        @pl.when(holds)
        def _():
            act()

    for half in range(2):
        keep[1 + half].wait()
        keep[3 + half].wait()
        for way in (0, 1):
            when(goes_on(way), lambda: w_line(way, 0, half).start())
    for i in range(3):
        mod_to(i).start()
    for part in range(parts):
        hid_to(1, across, part).start()
    for part in range(parts):
        hid_to(0, twin, part).start()
    for i in (1, 2, 0):
        q_to(i).start()

    def pass_weights(way, d, half):
        def act():
            w_arrived(way, d, half).wait_recv()
            if d < fsdp - 1:
                when(goes_on(way), lambda: w_line(way, d, half).start())
            w_swap(way, d, half).start()

        when(exists(way, d), act)

    def pass_hidden(part):
        hid_got(1, across, part).wait_recv()
        hid_relay(part).start()

    def send_ahead(unit, way, d):
        when(jnp.logical_and(has_ahead, groups[unit] >= 1), lambda: kv_ahead(unit, way, d).start())

    def pass_kv(unit, way, d):
        def act():
            kv_arrived(unit, way, d).wait_recv()
            if d < fsdp - 1:
                when(goes_on(way), lambda: kv_line(unit, way, d).start())
            send_ahead(unit, way, d)

        when(exists(way, d), act)

    def project(unit):
        group = groups[unit]
        image = jnp.max(mods[group]) == 1
        total = None
        for zs in range(fsdp):
            halves = [jnp.where(image, w[zs, 1, half], w[zs, 0, half]) for half in range(2)]
            weight = jnp.concatenate(halves, axis=1)
            rows_at = hid[group, :, zs * depth : (zs + 1) * depth]
            term = jnp.dot(rows_at, weight, preferred_element_type=jnp.float32)
            total = term if total is None else total + term
        rounded = total.astype(jnp.bfloat16)
        made[unit, 0] = rounded[:, :HD]
        made[unit, 1] = rounded[:, HD:]

    def send_made(unit):
        for way in (0, 1):
            when(goes_on(way), lambda: kv_line(unit, way, 0).start())
        send_ahead(unit, 0, 0)
        kv_keep(unit).start()

    docs_in.wait()
    starts[...], ends[...] = bounds(docs[...])
    mod_in.wait()
    for i in range(3):
        mod_got(i).wait_recv()
    block = hidden_ref.shape[0] * fsdp
    origin = (base - SPAN) * block
    for slot in range(QUAD):
        group = flip(s, slot)
        image = mods[group - base, :1] == 1
        for i in range(hidden_ref.shape[0] // LINE):
            first = group * block + z * hidden_ref.shape[0] + i * LINE
            line = lax.div(first, LINE)
            at = slice(i * LINE, (i + 1) * LINE)
            place = first + lax.broadcasted_iota(jnp.int32, (1, LINE), 1)
            last = jnp.minimum(ends[pl.ds(line, 1), :], group * block + block - 1)
            limits[slot : slot + 1, at] = starts[pl.ds(line, 1), :] - origin
            limits[QUAD + slot : QUAD + slot + 1, at] = jnp.where(image, last, place) - origin

    done = 0
    for d in range(1, fsdp):
        for half in range(2):
            for way in (0, 1):
                pass_weights(way, d, half)
        if done < parts - 2:
            pass_hidden(done)
            done += 1
    keep[0].wait()
    for part in range(parts):
        hid_got(0, twin, part).wait_recv()
    for way, d in lines:
        for half in range(2):
            when(exists(way, d), lambda: w_swapped(way, d, half).wait_recv())
    project(0)
    q_in.wait()
    q_keep.start()
    project(1)
    send_made(0)
    send_made(1)

    def relay(unit, d):
        for way in (0, 1):
            pass_kv(unit, way, d)

    pass_hidden(parts - 2)
    relay(0, 1)
    relay(1, 1)
    pass_hidden(parts - 1)
    relay(0, 2)
    for part in range(parts):
        hid_got(2, diag, part).wait_recv()
    project(2)
    project(3)
    send_made(2)
    send_made(3)
    for d in range(3, fsdp):
        relay(0, d)

    def relay_late():
        for d in range(1, fsdp):
            relay(2, d)
            relay(3, d)

    when(side == 0, relay_late)
    for d in range(2, fsdp):
        relay(1, d)
    when(side == 1, relay_late)
    for i in range(3):
        q_got(i).wait_recv()
    for unit in range(QUAD):
        for way, d in [(0, 0)] + lines:
            holds = jnp.logical_and(has_behind, groups[unit] >= 1)
            if d:
                holds = jnp.logical_and(holds, exists(way, d))
            when(holds, lambda: kv_behind(unit, way, d).wait_recv())

    q_keep.wait()
    for unit in range(QUAD):
        kv_keep(unit).wait()
    for half in range(2):
        for way in (0, 1):
            when(goes_on(way), lambda: w_line(way, 0, half).wait_send())
            for d in range(1, fsdp):
                def act(way=way, d=d, half=half):
                    if d < fsdp - 1:
                        when(goes_on(way), lambda: w_line(way, d, half).wait_send())
                    w_swap(way, d, half).wait_send()

                when(exists(way, d), act)
    for i in range(3):
        mod_to(i).wait_send()
        q_to(i).wait_send()
    for part in range(parts):
        hid_to(0, twin, part).wait_send()
        hid_to(1, across, part).wait_send()
        hid_relay(part).wait_send()

    def sent_ahead(unit, way, d):
        when(jnp.logical_and(has_ahead, groups[unit] >= 1), lambda: kv_ahead(unit, way, d).wait_send())

    for unit in range(QUAD):
        for way in (0, 1):
            when(goes_on(way), lambda: kv_line(unit, way, 0).wait_send())
        sent_ahead(unit, 0, 0)
        for way, d in lines:
            def act(unit=unit, way=way, d=d):
                if d < fsdp - 1:
                    when(goes_on(way), lambda: kv_line(unit, way, d).wait_send())
                sent_ahead(unit, way, d)

            when(exists(way, d), act)


def shifted(x, by, axis, fill):
    size = x.shape[axis]
    place = lax.broadcasted_iota(jnp.int32, x.shape, axis)
    moved = pltpu.roll(x, by % size, axis)
    inside = place >= by if by > 0 else place < size + by
    return jnp.where(inside, moved, fill)


def spread(x, pick, sign, fill):
    by = 1
    while by < x.shape[1]:
        x = pick(x, shifted(x, sign * by, 1, fill))
        by *= 2
    edge = x[:, -1:] if sign > 0 else x[:, :1]
    rows = shifted(jnp.broadcast_to(edge, x.shape), sign, 0, fill)
    by = 1
    while by < x.shape[0]:
        rows = pick(rows, shifted(rows, sign * by, 0, fill))
        by *= 2
    return pick(x, rows)


def bounds(docs):
    count = docs.shape[0] * docs.shape[1]
    place = (
        lax.broadcasted_iota(jnp.int32, docs.shape, 0) * docs.shape[1]
        + lax.broadcasted_iota(jnp.int32, docs.shape, 1)
    )
    lane = lax.broadcasted_iota(jnp.int32, docs.shape, 1)
    width = docs.shape[1]
    turned = pltpu.roll(docs, 1, 1)
    before = jnp.where(lane == 0, shifted(turned, 1, 0, -1), turned)
    turned = pltpu.roll(docs, width - 1, 1)
    after = jnp.where(lane == width - 1, shifted(turned, -1, 0, -1), turned)
    starts = jnp.where(docs != before, place, 0)
    ends = jnp.where(docs != after, place, count - 1)
    return spread(starts, jnp.maximum, 1, 0), spread(ends, jnp.minimum, -1, count - 1)


def gather(hidden, queries, kv_weights, image_groups, doc_ids):
    seq, fsdp = lax.axis_size("seq"), lax.axis_size("fsdp")
    rows, width = hidden.shape
    depth = kv_weights.shape[1]
    parts = 4
    marked = jnp.broadcast_to(image_groups[0], (8, LINE))
    docs = doc_ids.reshape(-1, LINE)
    anywhere = pl.BlockSpec(memory_space=pl.ANY)
    far = pl.BlockSpec(memory_space=pltpu.HBM)
    vmem = pl.BlockSpec(memory_space=pltpu.VMEM)
    dma = pltpu.SemaphoreType.DMA
    bf16 = jnp.bfloat16
    return pl.pallas_call(
        functools.partial(gather_kernel, seq, fsdp, parts),
        in_specs=[far] * 5,
        out_specs=[anywhere, anywhere, vmem],
        out_shape=[
            jax.ShapeDtypeStruct((2, SPAN + QUAD, fsdp, rows, HD), bf16),
            jax.ShapeDtypeStruct((QUAD, rows, WIDE), bf16),
            jax.ShapeDtypeStruct((2 * QUAD, rows), jnp.int32),
        ],
        scratch_shapes=[
            pltpu.VMEM((QUAD, rows, width), bf16),
            pltpu.VMEM((fsdp, 2, 2, depth, HD), bf16),
            pltpu.VMEM((QUAD, 2, rows, HD), bf16),
            pltpu.VMEM((QUAD, 8, LINE), jnp.int32),
            pltpu.VMEM((rows, WIDE), bf16),
            pltpu.VMEM(docs.shape, jnp.int32),
            pltpu.VMEM(docs.shape, jnp.int32),
            pltpu.VMEM(docs.shape, jnp.int32),
            dma((9,)),
            dma((3, parts)),
            dma((3, parts)),
            dma((3,)),
            dma((3,)),
            dma((3,)),
            dma((3,)),
            dma((2, fsdp, 2)),
            dma((2, fsdp + 1, 2)),
            dma((2, fsdp, 2)),
            dma((2, fsdp, 2)),
            dma((QUAD, 2, fsdp)),
            dma((QUAD, 2, fsdp + 1)),
            dma((QUAD, 2 * fsdp)),
            dma((QUAD, 2 * fsdp)),
            dma((QUAD,)),
        ],
        compiler_params=pltpu.CompilerParams(
            collective_id=0, has_side_effects=True, vmem_limit_bytes=32 * 1024 * 1024
        ),
        name="gather",
    )(marked, *(pltpu.with_memory_space_constraint(x, pltpu.HBM) for x in (docs, hidden, kv_weights, queries)))


def attend_kernel(key_block, slot, limits_ref, q_ref, k_ref, after_ref, out_ref, qt, top, total, acc):
    rows = q_ref.shape[1]
    lo_ref = limits_ref.at[slot : slot + 1]
    hi_ref = limits_ref.at[QUAD + slot : QUAD + slot + 1]
    lo, hi = lo_ref[...], hi_ref[...]
    lo_min, lo_max, hi_min, hi_max = jnp.min(lo), jnp.max(lo), jnp.min(hi), jnp.max(hi)
    first = lax.div(lo_min, key_block)
    end = lax.div(hi_max, key_block) + 1
    full_first = jnp.minimum(lax.div(lo_max + key_block - 1, key_block), end)
    full_end = jnp.maximum(lax.div(hi_min + 1, key_block), full_first)

    lanes = [slice(g * rows, (g + 1) * rows) for g in range(PER)]
    factor = math.log2(math.e) / math.sqrt(HD)
    for g in range(PER):
        qt[:, g * rows : (g + 1) * rows] = q_ref[slot, :, g * HD : (g + 1) * HD].T
    top[...] = jnp.full_like(top, NEG)
    total[...] = jnp.zeros_like(total)
    acc[...] = jnp.zeros_like(acc)

    def step(masked, b, _):
        at = pl.multiple_of(b * key_block, key_block)
        keys = k_ref[0, pl.ds(at, key_block), :]
        values = k_ref[1, pl.ds(at, key_block), :]
        if masked:
            place = at + lax.broadcasted_iota(jnp.int32, (key_block, rows), 0)
            allowed = jnp.logical_and(place >= lo_ref[...], place <= hi_ref[...])
        scores = [jnp.dot(keys, qt[:, at_g], preferred_element_type=jnp.float32) for at_g in lanes]
        if masked:
            scores = [jnp.where(allowed, score, NEG) for score in scores]
        before = [top[:, at_g] for at_g in lanes]
        peak = [
            jnp.maximum(old, jnp.max(score, axis=0, keepdims=True))
            for old, score in zip(before, scores)
        ]
        weights = [jnp.exp2((score - high) * factor) for score, high in zip(scores, peak)]
        shrink = [jnp.exp2((old - high) * factor) for old, high in zip(before, peak)]
        added = [jnp.sum(weight, axis=0, keepdims=True) for weight in weights]
        mixed = [
            lax.dot_general(
                values,
                weight.astype(jnp.bfloat16),
                (((0,), (0,)), ((), ())),
                preferred_element_type=jnp.float32,
            )
            for weight in weights
        ]
        for g, at_g in enumerate(lanes):
            top[:, at_g] = peak[g]
            total[:, at_g] = total[:, at_g] * shrink[g] + added[g]
            acc[:, at_g] = acc[:, at_g] * shrink[g] + mixed[g]
        return 0

    lax.fori_loop(first, full_first, functools.partial(step, True), 0)
    lax.fori_loop(full_first, full_end, functools.partial(step, False), 0)
    lax.fori_loop(full_end, end, functools.partial(step, True), 0)
    for g in range(PER):
        mixed = (acc[:, lanes[g]] / total[:, lanes[g]]).T
        out_ref[:, g * HD : (g + 1) * HD] = mixed.astype(out_ref.dtype)


def attend(kv, queries, limits, after, slot):
    fsdp = lax.axis_size("fsdp")
    _, rows, wide = queries.shape
    n_keys = kv.shape[1] * kv.shape[2] * kv.shape[3]
    kv = kv.reshape(2, n_keys, HD)
    key_block = math.gcd(rows * fsdp, 512)
    vmem = pl.BlockSpec(memory_space=pltpu.VMEM)
    work = rows * PER * n_keys // 4
    return pl.pallas_call(
        functools.partial(attend_kernel, key_block, slot),
        in_specs=[vmem] * 3 + [pl.BlockSpec(memory_space=pl.ANY)],
        out_specs=vmem,
        out_shape=jax.ShapeDtypeStruct((rows, wide), queries.dtype),
        scratch_shapes=[
            pltpu.VMEM((HD, PER * rows), jnp.bfloat16),
            pltpu.VMEM((1, PER * rows), jnp.float32),
            pltpu.VMEM((1, PER * rows), jnp.float32),
            pltpu.VMEM((HD, PER * rows), jnp.float32),
        ],
        compiler_params=pltpu.CompilerParams(vmem_limit_bytes=16 * 1024 * 1024),
        cost_estimate=pl.CostEstimate(flops=4 * HD * work, bytes_accessed=4 * HD * n_keys, transcendentals=work),
    )(limits, queries, kv, after)


def assemble_kernel(*refs):
    h = lax.axis_index("seq") % QUAD
    out_ref, sems = refs[QUAD:]
    wide = refs[0].shape[1]
    copies = [
        pltpu.make_async_copy(
            refs[slot], out_ref.at[:, pl.ds(pl.multiple_of(flip(h, slot) * wide, HD), wide)], sems.at[slot]
        )
        for slot in range(QUAD)
    ]
    for copy in copies:
        copy.start()
    for copy in copies:
        copy.wait()


def assemble(pieces):
    rows, wide = pieces[0].shape
    return pl.pallas_call(
        assemble_kernel,
        in_specs=[pl.BlockSpec(memory_space=pltpu.VMEM)] * QUAD,
        out_specs=pl.BlockSpec(memory_space=pl.ANY),
        out_shape=jax.ShapeDtypeStruct((rows, QUAD * wide), pieces[0].dtype),
        scratch_shapes=[pltpu.SemaphoreType.DMA((QUAD,))],
        compiler_params=pltpu.CompilerParams(vmem_limit_bytes=8 * 1024 * 1024),
        name="assemble",
    )(*pieces)


def local(hidden, queries, kv_weights, image_groups, doc_ids):
    seq = lax.axis_size("seq")
    kv, q, limits = gather(hidden, queries, kv_weights, image_groups, doc_ids)
    pieces = [None] * QUAD
    mixed = limits
    for slot in (3, 2, 1, 0):
        mixed = attend(kv, q, limits, mixed, slot)
        swap = [(i, i ^ slot) for i in range(seq)]
        pieces[slot] = lax.ppermute(mixed, "seq", swap) if slot else mixed
    return assemble(pieces)


def solution(mesh):
    in_specs = (
        P(("seq", "fsdp"), None),
        P(("seq", "fsdp"), None),
        P(None, "fsdp", None),
        P("seq"),
        P(),
    )
    out_specs = P(("seq", "fsdp"), None)
    return jax.shard_map(local, mesh=mesh, in_specs=in_specs, out_specs=out_specs, check_vma=False)
```
